32 devices in a mesh: near: 4 (over x, core), far: 8 (over z, y).
Axes of the slice: x: 2, y: 2, z: 4, core: 2. Of those that a mesh axis runs over, the one named last changes fastest.
Arguments:
- w_reduce: bfloat16 [4, 8, 256, 1024], P('near', 'far'), may hold values from -6 to 6
- w_expand: bfloat16 [4, 8, 256, 1024], P('near', 'far'), may hold values from -6 to 6
- inputs: bfloat16 [4, 8, 2, 256, 1024], P('near', 'far'), may hold values from -6 to 6
- out_grads: bfloat16 [4, 8, 2, 256, 1024], P('near', 'far'), may hold values from -12 to 12
Outputs:
- new_reduce: float32 [4, 8, 256, 1024], P('near', 'far')
- new_expand: float32 [4, 8, 256, 1024], P('near', 'far')
The draws below stay inside these ranges and needn't reach their ends.
All inputs are finite; a program needn't handle non-finite values.
Results may differ from the reference program's by a relative error of at most 0.0003.
Values sent between devices are 32-bit elements; how exact they have to be, the bound alone decides.
No kernel may reach another device: no remote copies, remote signals or barrier semaphores. Data moves between devices by JAX's collectives and lax.ppermute only.
A program may use at most 64 MiB of HBM per device.

```python
import jax
import jax.numpy as jnp
import numpy as np
from jax import lax

C = 1024
B = 256
ROWS = 256
ITERS = 2
NEARS = 4
FARS = 8


def levels(own_key, shape, split, low, high):
    gain, own = 1.0, jax.random.fold_in(own_key, 6)
    for dim, parts in split:
        draws = jnp.exp(jax.random.uniform(jax.random.fold_in(own, dim), (parts,), jnp.float32, low / len(split), high / len(split)))
        gain = gain * jnp.repeat(draws, shape[dim] // parts).reshape([-1 if axis == dim else 1 for axis in range(len(shape))])
    return gain


def normal_values(rng, extent, scale, reach, cuts=(), dtype=jnp.bfloat16):
    loudness = levels(rng, extent, cuts, -0.22, 0.18) if cuts else 1.0
    result = jax.random.normal(rng, extent, jnp.float32) * scale * loudness
    return jnp.minimum(jnp.maximum(result, -reach), reach).astype(dtype)


def setup_inputs(seed: int = 0) -> dict:
    seeds = jax.random.split(jax.random.key(seed), 5)
    w_reduce = normal_values(seeds[0], (NEARS, FARS, B, C), 1.0, 6.0, ((0, 4), (1, 8)))
    w_expand = normal_values(seeds[1], (NEARS, FARS, B, C), 1.0, 6.0, ((0, 4), (1, 8)))
    inputs = normal_values(seeds[2], (NEARS, FARS, ITERS, ROWS, C), 1.0, 6.0, ((0, 4), (1, 8)))
    out_grads = normal_values(seeds[3], (NEARS, FARS, ITERS, ROWS, C), 2.0, 12.0, ((0, 4), (1, 8)))
    return {"w_reduce": w_reduce, "w_expand": w_expand, "inputs": inputs, "out_grads": out_grads}


learn_rate = 1.0

def smooth_grad(values):
    sig = jax.nn.sigmoid(values)
    return sig * (1.0 + values * (1.0 - sig))

def local_step(reducing, expanding, pixels, upstream):
    highest = lax.Precision.HIGHEST
    reduce_scale = 1.0 / np.sqrt(C)
    expand_scale = 1.0 / np.sqrt(B)
    feats = pixels.astype(jnp.float32)
    grads = upstream.astype(jnp.float32)
    pre_act = jnp.dot(feats, reducing.T, precision=highest) * reduce_scale
    hidden = jax.nn.silu(pre_act)
    summed = feats + jnp.dot(hidden, expanding, precision=highest) * expand_scale
    grad_sum = grads * smooth_grad(summed)
    grad_expand = jnp.dot(hidden.T, grad_sum, precision=highest) * expand_scale
    grad_hidden = jnp.dot(grad_sum, expanding.T, precision=highest) * expand_scale
    grad_pre = grad_hidden * smooth_grad(pre_act)
    grad_reduce = jnp.dot(grad_pre.T, feats, precision=highest) * reduce_scale
    return (reducing - learn_rate * grad_reduce, expanding - learn_rate * grad_expand)

def reference(w_reduce, w_expand, inputs, out_grads):
    reducing = w_reduce.astype(jnp.float32).reshape(NEARS * FARS, B, C)
    expanding = w_expand.astype(jnp.float32).reshape(NEARS * FARS, B, C)
    pixels = inputs.reshape(NEARS * FARS, ITERS, ROWS, C)
    upstream = out_grads.reshape(NEARS * FARS, ITERS, ROWS, C)
    for iteration in range(ITERS):
        reducing, expanding = jax.vmap(local_step)(reducing, expanding, pixels[:, iteration], upstream[:, iteration])
        both = jnp.stack([reducing.reshape(NEARS, FARS, B, C), expanding.reshape(NEARS, FARS, B, C)])
        for bit_index in range(2):
            partner = np.arange(NEARS) ^ 1 << bit_index
            both = (both + both[:, partner]) * 0.5
        for bit_index in range(2):
            partner = np.arange(FARS) ^ 1 << bit_index
            both = (both + both[:, :, partner]) * 0.5
        reducing = both[0].reshape(NEARS * FARS, B, C)
        expanding = both[1].reshape(NEARS * FARS, B, C)
    return (reducing.reshape(NEARS, FARS, B, C), expanding.reshape(NEARS, FARS, B, C))
```

```python
import math

import jax
import jax.numpy as jnp
from jax import lax
from jax.sharding import PartitionSpec as P

learn_rate = 1.0

ORDERS = (
    ((1, 2, 3), (2, 3, 1)),
    ((3, 1, 2), (1, 2, 3)),
    ((2, 3, 1), (3, 1, 2)),
    ((1, 2, 3), (2, 3, 1)),
)


def own_bits():
    near, far = lax.axis_index("near"), lax.axis_index("far")
    return (near & 1, (near >> 1) & 1, far & 1, (far >> 1) & 1)


def from_partner(values, even_bit, odd_bit):
    nears, fars = lax.axis_size("near"), lax.axis_size("far")
    pairs = []
    for near in range(nears):
        for far in range(fars):
            bit = odd_bit if near & 1 else even_bit
            to_near = near ^ (1 << bit) if bit < 2 else near
            to_far = far ^ (1 << (bit - 2)) if bit >= 2 else far
            pairs.append((near * fars + far, to_near * fars + to_far))
    return lax.ppermute(values, ("near", "far"), pairs)


def split(values, bit):
    rows = values.shape[0] // 2
    low, high = values[:rows], values[rows:]
    return jnp.where(bit == 0, low, high), jnp.where(bit == 0, high, low)


def join(own, other, bit):
    return jnp.concatenate([jnp.where(bit == 0, own, other), jnp.where(bit == 0, other, own)])


def sum_over_cube(values, order, bits):
    even, odd = order
    core = bits[0]
    first = jnp.where(core == 0, bits[even[0]], bits[odd[0]])
    first_over = jnp.where(core == 0, bits[odd[0]], bits[even[0]])
    keep, send = split(values, core)
    total = keep + from_partner(send, 0, 0)
    keep, send = split(total, first)
    total = keep + from_partner(send, even[0], odd[0])
    total = total + from_partner(total, even[1], odd[1])
    total = total + from_partner(total, even[2], odd[2])
    total_over = from_partner(total, 0, 0)
    rest = from_partner(total, even[0], odd[0])
    rest_over = from_partner(rest, 0, 0)
    return join(join(total, rest, first), join(total_over, rest_over, first_over), core)


def smooth_grad(values):
    sig = jax.nn.sigmoid(values)
    return sig * (1.0 + values * (1.0 - sig))


def average(reducing, expanding, bits):
    columns = expanding.shape[1] // 2
    rows = reducing.shape[0] // 2
    parts = (expanding[:, :columns], expanding[:, columns:], reducing[:rows], reducing[rows:])
    parts = [sum_over_cube(part * 0.0625, order, bits) for part, order in zip(parts, ORDERS)]
    return jnp.concatenate(parts[2:], axis=0), jnp.concatenate(parts[:2], axis=1)


def shards(w_reduce, w_expand, inputs, out_grads):
    highest = lax.Precision.HIGHEST
    bits = own_bits()
    reducing = w_reduce[0, 0].astype(jnp.float32)
    expanding = w_expand[0, 0].astype(jnp.float32)
    reduce_scale = 1.0 / math.sqrt(reducing.shape[1])
    expand_scale = 1.0 / math.sqrt(reducing.shape[0])
    for iteration in range(inputs.shape[2]):
        feats = inputs[0, 0, iteration].astype(jnp.float32)
        grads = out_grads[0, 0, iteration].astype(jnp.float32)
        pre_act = jnp.dot(feats, reducing.T, precision=highest) * reduce_scale
        hidden = jax.nn.silu(pre_act)
        summed = feats + jnp.dot(hidden, expanding, precision=highest) * expand_scale
        grad_sum = grads * smooth_grad(summed)
        grad_expand = jnp.dot(hidden.T, grad_sum, precision=highest) * expand_scale
        grad_hidden = jnp.dot(grad_sum, expanding.T, precision=highest) * expand_scale
        expanding = expanding - learn_rate * grad_expand
        grad_pre = grad_hidden * smooth_grad(pre_act)
        grad_reduce = jnp.dot(grad_pre.T, feats, precision=highest) * reduce_scale
        reducing = reducing - learn_rate * grad_reduce
        reducing, expanding = average(reducing, expanding, bits)
    return (reducing[None, None], expanding[None, None])


def solution(mesh):
    in_specs = (
        P("near", "far", None, None),
        P("near", "far", None, None),
        P("near", "far", None, None, None),
        P("near", "far", None, None, None),
    )
    out_specs = (P("near", "far", None, None), P("near", "far", None, None))
    return jax.shard_map(shards, mesh=mesh, in_specs=in_specs, out_specs=out_specs, check_vma=False)
```

```python
import functools
import math

import jax
import jax.numpy as jnp
from jax import lax
from jax.experimental import pallas as pl
from jax.experimental.pallas import tpu as pltpu
from jax.sharding import PartitionSpec as P

learn_rate = 1.0

ORDERS = (
    ((1, 2, 3), (2, 3, 1)),
    ((3, 1, 2), (1, 2, 3)),
    ((2, 3, 1), (3, 1, 2)),
    ((1, 2, 3), (2, 3, 1)),
)
BITS = 4
VMEM_LIMIT = 24 * 2**20
f32, bf16 = jnp.float32, jnp.bfloat16


def own_bits():
    near, far = lax.axis_index("near"), lax.axis_index("far")
    return (near & 1, (near >> 1) & 1, far & 1, (far >> 1) & 1)


def from_partner(values, even_bit, odd_bit):
    nears, fars = lax.axis_size("near"), lax.axis_size("far")
    pairs = []
    for near in range(nears):
        for far in range(fars):
            bit = odd_bit if near & 1 else even_bit
            to_near = near ^ (1 << bit) if bit < 2 else near
            to_far = far ^ (1 << (bit - 2)) if bit >= 2 else far
            pairs.append((near * fars + far, to_near * fars + to_far))
    return lax.ppermute(values, ("near", "far"), pairs)


def split(values, bit):
    rows = values.shape[0] // 2
    low, high = values[:rows], values[rows:]
    return jnp.where(bit == 0, low, high), jnp.where(bit == 0, high, low)


def join(own, other, bit):
    return jnp.concatenate([jnp.where(bit == 0, own, other), jnp.where(bit == 0, other, own)])


def chain(total, order, bits):
    even, odd = order
    first = jnp.where(bits[0] == 0, bits[even[0]], bits[odd[0]])
    keep, send = split(total, first)
    own = keep + from_partner(send, even[0], odd[0])
    own = own + from_partner(own, even[1], odd[1])
    own = own + from_partner(own, even[2], odd[2])
    return join(own, from_partner(own, even[0], odd[0]), first)


def sum_over_cube(keep, send, orders, bits):
    total = keep + from_partner(send, 0, 0)
    rows = total.shape[0] // len(orders)
    parts = [chain(total[rows * k : rows * (k + 1)], order, bits) for k, order in enumerate(orders)]
    over = [from_partner(part, 0, 0) for part in parts]
    return join(jnp.concatenate(parts), jnp.concatenate(over), bits[0])


def halves(values):
    high = values.astype(bf16)
    return high, (values - high.astype(f32)).astype(bf16)


def product(left, right, contract):
    total = None
    for i, a in enumerate(left):
        for j, b in enumerate(right):
            if i + j < 2:
                term = lax.dot_general(a, b, (contract, ((), ())), preferred_element_type=f32)
                total = term if total is None else total + term
    return total


def parts_of(values):
    return (values,) if values.dtype == bf16 else halves(values)


NN = ((1,), (0,))
NT = ((1,), (1,))


def expand_kernel(iteration, core_ref, x_hbm, g_hbm, r_ref, e_ref, keep_ref, send_ref, zh_ref, zl_ref, slope_ref, x_ref, g_ref, sems):
    copy_x = pltpu.make_async_copy(x_hbm.at[iteration], x_ref, sems.at[0])
    copy_g = pltpu.make_async_copy(g_hbm.at[iteration], g_ref, sems.at[1])
    copy_x.start()
    copy_g.start()
    width, columns = r_ref.shape
    reduce_scale = 1.0 / math.sqrt(columns)
    expand_scale = 1.0 / math.sqrt(width)
    copy_x.wait()
    feats = x_ref[...]
    pre = product(parts_of(r_ref[...]), (feats,), NT) * reduce_scale
    sig = jax.nn.sigmoid(pre)
    hidden = pre * sig
    slope_ref[...] = sig * (1.0 + pre * (1.0 - sig))
    hidden_t = halves(hidden)
    hidden_n = halves(hidden.T)
    e_parts = parts_of(e_ref[...])
    summed = feats.astype(f32) + product(hidden_n, e_parts, NN) * expand_scale
    copy_g.wait()
    sig = jax.nn.sigmoid(summed)
    grads = halves(g_ref[...].astype(f32) * (sig * (1.0 + summed * (1.0 - sig))))
    zh_ref[...] = grads[0]
    zl_ref[...] = grads[1]
    stepped = (e_ref[...].astype(f32) - learn_rate * expand_scale * product(hidden_t, grads, NN)) * (0.5**BITS)
    rows = width // 2
    even = core_ref[0] == 0
    keep_ref[...] = jnp.where(even, stepped[:rows], stepped[rows:])
    send_ref[...] = jnp.where(even, stepped[rows:], stepped[:rows])


def reduce_kernel(iteration, core_ref, x_hbm, r_ref, e_ref, zh_ref, zl_ref, slope_ref, keep_ref, send_ref, x_ref, sems):
    copy_x = pltpu.make_async_copy(x_hbm.at[iteration], x_ref, sems.at[0])
    copy_x.start()
    width, columns = r_ref.shape
    reduce_scale = 1.0 / math.sqrt(columns)
    expand_scale = 1.0 / math.sqrt(width)
    grad_hidden = product(parts_of(e_ref[...]), (zh_ref[...], zl_ref[...]), NT) * expand_scale
    grad_pre = halves(grad_hidden * slope_ref[...])
    copy_x.wait()
    stepped = (r_ref[...].astype(f32) - learn_rate * reduce_scale * product(grad_pre, (x_ref[...],), NN)) * (0.5**BITS)
    rows = width // 2
    even = core_ref[0] == 0
    keep_ref[...] = jnp.where(even, stepped[:rows], stepped[rows:])
    send_ref[...] = jnp.where(even, stepped[rows:], stepped[:rows])


def local_step(iteration, core, inputs, out_grads, reducing, expanding):
    rows, columns = inputs.shape[1:]
    width = reducing.shape[0]
    vmem = pl.BlockSpec(memory_space=pltpu.VMEM)
    smem = pl.BlockSpec(memory_space=pltpu.SMEM)
    anywhere = pl.BlockSpec(memory_space=pl.ANY)
    half = jax.ShapeDtypeStruct((width // 2, columns), f32)
    grads = jax.ShapeDtypeStruct((rows, columns), bf16)
    keep_e, send_e, zh, zl, slope = pl.pallas_call(
        functools.partial(expand_kernel, iteration),
        out_shape=(half, half, grads, grads, jax.ShapeDtypeStruct((width, rows), f32)),
        in_specs=[smem, anywhere, anywhere, vmem, vmem],
        out_specs=(vmem,) * 5,
        scratch_shapes=[pltpu.VMEM((rows, columns), bf16), pltpu.VMEM((rows, columns), bf16), pltpu.SemaphoreType.DMA((2,))],
        compiler_params=pltpu.CompilerParams(vmem_limit_bytes=VMEM_LIMIT),
        name=f"expand_{iteration}",
    )(core, inputs, out_grads, reducing, expanding)
    keep_r, send_r = pl.pallas_call(
        functools.partial(reduce_kernel, iteration),
        out_shape=(half, half),
        in_specs=[smem, anywhere, vmem, vmem, vmem, vmem, vmem],
        out_specs=(vmem,) * 2,
        scratch_shapes=[pltpu.VMEM((rows, columns), bf16), pltpu.SemaphoreType.DMA((1,))],
        compiler_params=pltpu.CompilerParams(vmem_limit_bytes=VMEM_LIMIT),
        name=f"reduce_{iteration}",
    )(core, inputs, reducing, expanding, zh, zl, slope)
    return keep_r, send_r, keep_e, send_e


def shards(w_reduce, w_expand, inputs, out_grads):
    bits = own_bits()
    core = bits[0].astype(jnp.int32).reshape(1)
    reducing, expanding = w_reduce[0, 0], w_expand[0, 0]
    for iteration in range(inputs.shape[2]):
        keep_r, send_r, keep_e, send_e = local_step(iteration, core, inputs[0, 0], out_grads[0, 0], reducing, expanding)
        expanding = sum_over_cube(keep_e, send_e, ORDERS[:2], bits)
        reducing = sum_over_cube(keep_r, send_r, ORDERS[2:], bits)
    return (reducing[None, None], expanding[None, None])


def solution(mesh):
    in_specs = (
        P("near", "far", None, None),
        P("near", "far", None, None),
        P("near", "far", None, None, None),
        P("near", "far", None, None, None),
    )
    out_specs = (P("near", "far", None, None), P("near", "far", None, None))
    return jax.shard_map(shards, mesh=mesh, in_specs=in_specs, out_specs=out_specs, check_vma=False)
```

```python
import functools
import math

import jax
import jax.numpy as jnp
from jax import lax
from jax.experimental import pallas as pl
from jax.experimental.pallas import tpu as pltpu
from jax.sharding import PartitionSpec as P

learn_rate = 1.0

ORDERS = (
    ((1, 2, 3), (2, 3, 1)),
    ((3, 1, 2), (1, 2, 3)),
    ((2, 3, 1), (3, 1, 2)),
    ((1, 2, 3), (2, 3, 1)),
)
BITS = 4
VMEM_LIMIT = 24 * 2**20
f32, bf16 = jnp.float32, jnp.bfloat16


def bits_of(near, far):
    chip = ((near >> 1) & 1, far & 1, (far >> 1) & 1)
    return ((near & 1) ^ chip[0] ^ chip[1] ^ chip[2],) + chip


def from_partner(values, *bit_of_role):
    nears, fars = lax.axis_size("near"), lax.axis_size("far")
    pairs = []
    for near in range(nears):
        for far in range(fars):
            bit = bit_of_role[bits_of(near, far)[0]]
            to_near = near ^ 1 ^ (2 if bit == 1 else 0)
            to_far = far ^ (1 << (bit - 2)) if bit >= 2 else far
            pairs.append((near * fars + far, to_near * fars + to_far))
    return lax.ppermute(values, ("near", "far"), pairs)


def split(values, bit):
    rows = values.shape[0] // 2
    low, high = values[:rows], values[rows:]
    return jnp.where(bit == 0, low, high), jnp.where(bit == 0, high, low)


def join(own, other, bit):
    return jnp.concatenate([jnp.where(bit == 0, own, other), jnp.where(bit == 0, other, own)])


def chain(total, order, bits):
    even, odd = order
    first = jnp.where(bits[0] == 0, bits[even[0]], bits[odd[0]])
    keep, send = split(total, first)
    own = keep + from_partner(send, even[0], odd[0])
    own = own + from_partner(own, even[1], odd[1])
    own = own + from_partner(own, even[2], odd[2])
    return join(own, from_partner(own, even[0], odd[0]), first)


def sum_over_cube(keep, send, orders, bits):
    total = keep + from_partner(send, 0, 0)
    rows = total.shape[0] // len(orders)
    parts = [chain(total[rows * k : rows * (k + 1)], order, bits) for k, order in enumerate(orders)]
    over = [from_partner(part, 0, 0) for part in parts]
    return join(jnp.concatenate(parts), jnp.concatenate(over), bits[0])


def halves(values):
    high = values.astype(bf16)
    return high, (values - high.astype(f32)).astype(bf16)


def product(left, right, contract):
    total = None
    for i, a in enumerate(left):
        for j, b in enumerate(right):
            if i + j < 2:
                term = lax.dot_general(a, b, (contract, ((), ())), preferred_element_type=f32)
                total = term if total is None else total + term
    return total


def parts_of(values):
    return (values,) if values.dtype == bf16 else halves(values)


NN = ((1,), (0,))
NT = ((1,), (1,))


def expand_kernel(first, role_ref, x_in, g_in, r_in, e_in, *refs):
    if first:
        keep_ref, send_ref, zh_ref, zl_ref, slope_ref, x_ref, r_ref, e_ref, g_ref, sems = refs
        copies = [
            pltpu.make_async_copy(source, target, sems.at[i])
            for i, (source, target) in enumerate(((r_in, r_ref), (x_in.at[0], x_ref), (e_in, e_ref), (g_in.at[0], g_ref)))
        ]
        for copy in copies:
            copy.start()
        copies[0].wait()
        copies[1].wait()
    else:
        keep_ref, send_ref, zh_ref, zl_ref, slope_ref = refs
        x_ref, g_ref, r_ref, e_ref = x_in, g_in, r_in, e_in
    width, columns = r_ref.shape
    reduce_scale = 1.0 / math.sqrt(columns)
    expand_scale = 1.0 / math.sqrt(width)
    feats = x_ref[...]
    pre = product(parts_of(r_ref[...]), (feats,), NT) * reduce_scale
    sig = jax.nn.sigmoid(pre)
    hidden = pre * sig
    slope_ref[...] = sig * (1.0 + pre * (1.0 - sig))
    hidden_t = halves(hidden)
    hidden_n = halves(hidden.T)
    if first:
        copies[2].wait()
    e_parts = parts_of(e_ref[...])
    summed = feats.astype(f32) + product(hidden_n, e_parts, NN) * expand_scale
    if first:
        copies[3].wait()
    sig = jax.nn.sigmoid(summed)
    grads = halves(g_ref[...].astype(f32) * (sig * (1.0 + summed * (1.0 - sig))))
    zh_ref[...] = grads[0]
    zl_ref[...] = grads[1]
    stepped = (e_ref[...].astype(f32) - learn_rate * expand_scale * product(hidden_t, grads, NN)) * (0.5**BITS)
    rows = width // 2
    even = role_ref[0] == 0
    keep_ref[...] = jnp.where(even, stepped[:rows], stepped[rows:])
    send_ref[...] = jnp.where(even, stepped[rows:], stepped[:rows])


def reduce_kernel(upcoming, role_ref, x_all, g_all, x_ref, r_ref, e_ref, zh_ref, zl_ref, slope_ref, keep_ref, send_ref, *refs):
    if upcoming is not None:
        next_x_ref, next_g_ref, sems = refs
        copies = (
            pltpu.make_async_copy(x_all.at[upcoming], next_x_ref, sems.at[0]),
            pltpu.make_async_copy(g_all.at[upcoming], next_g_ref, sems.at[1]),
        )
        for copy in copies:
            copy.start()
    width, columns = r_ref.shape
    reduce_scale = 1.0 / math.sqrt(columns)
    expand_scale = 1.0 / math.sqrt(width)
    grad_hidden = product(parts_of(e_ref[...]), (zh_ref[...], zl_ref[...]), NT) * expand_scale
    grad_pre = halves(grad_hidden * slope_ref[...])
    stepped = (r_ref[...].astype(f32) - learn_rate * reduce_scale * product(grad_pre, (x_ref[...],), NN)) * (0.5**BITS)
    rows = width // 2
    even = role_ref[0] == 0
    keep_ref[...] = jnp.where(even, stepped[:rows], stepped[rows:])
    send_ref[...] = jnp.where(even, stepped[rows:], stepped[:rows])
    if upcoming is not None:
        for copy in copies:
            copy.wait()


def shards(w_reduce, w_expand, inputs, out_grads):
    bits = bits_of(lax.axis_index("near"), lax.axis_index("far"))
    role = bits[0].astype(jnp.int32).reshape(1)
    reducing, expanding, inputs, out_grads = w_reduce[0, 0], w_expand[0, 0], inputs[0, 0], out_grads[0, 0]
    iterations, rows, columns = inputs.shape
    width = reducing.shape[0]
    vmem = pl.BlockSpec(memory_space=pltpu.VMEM)
    smem = pl.BlockSpec(memory_space=pltpu.SMEM)
    hbm = pl.BlockSpec(memory_space=pltpu.HBM)
    half = jax.ShapeDtypeStruct((width // 2, columns), f32)
    acts = jax.ShapeDtypeStruct((rows, columns), bf16)
    weights = jax.ShapeDtypeStruct((width, columns), bf16)
    slopes = jax.ShapeDtypeStruct((width, rows), f32)
    params = pltpu.CompilerParams(vmem_limit_bytes=VMEM_LIMIT)
    feats = grads = None
    for iteration in range(iterations):
        first, last = iteration == 0, iteration == iterations - 1
        expand = pl.pallas_call(
            functools.partial(expand_kernel, first),
            out_shape=(half, half, acts, acts, slopes) + ((acts, weights, weights) if first else ()),
            in_specs=[smem] + [hbm if first else vmem] * 4,
            out_specs=(vmem,) * (8 if first else 5),
            scratch_shapes=[pltpu.VMEM((rows, columns), bf16), pltpu.SemaphoreType.DMA((4,))] if first else [],
            compiler_params=params,
            name=f"expand_{iteration}",
        )
        if first:
            keep_e, send_e, zh, zl, slope, feats, reducing, expanding = expand(role, inputs, out_grads, reducing, expanding)
        else:
            keep_e, send_e, zh, zl, slope = expand(role, feats, grads, reducing, expanding)
        results = pl.pallas_call(
            functools.partial(reduce_kernel, None if last else iteration + 1),
            out_shape=(half, half) + (() if last else (acts, acts)),
            in_specs=[smem, hbm, hbm] + [vmem] * 6,
            out_specs=(vmem,) * (2 if last else 4),
            scratch_shapes=[] if last else [pltpu.SemaphoreType.DMA((2,))],
            compiler_params=params,
            name=f"reduce_{iteration}",
        )(role, inputs, out_grads, feats, reducing, expanding, zh, zl, slope)
        keep_r, send_r = results[:2]
        if not last:
            feats, grads = results[2:]
        expanding = sum_over_cube(keep_e, send_e, ORDERS[:2], bits)
        reducing = sum_over_cube(keep_r, send_r, ORDERS[2:], bits)
    return (reducing[None, None], expanding[None, None])


def solution(mesh):
    in_specs = (
        P("near", "far", None, None),
        P("near", "far", None, None),
        P("near", "far", None, None, None),
        P("near", "far", None, None, None),
    )
    out_specs = (P("near", "far", None, None), P("near", "far", None, None))
    return jax.shard_map(shards, mesh=mesh, in_specs=in_specs, out_specs=out_specs, check_vma=False)
```

```python
import functools
import math

import jax
import jax.numpy as jnp
from jax import lax
from jax.experimental import pallas as pl
from jax.experimental.pallas import tpu as pltpu
from jax.sharding import PartitionSpec as P

learn_rate = 1.0

ORDERS = (
    ((1, 2, 3), (2, 3, 1)),
    ((3, 1, 2), (1, 2, 3)),
    ((2, 3, 1), (3, 1, 2)),
    ((1, 2, 3), (2, 3, 1)),
)
BITS = 4
VMEM_LIMIT = 24 * 2**20
f32, bf16 = jnp.float32, jnp.bfloat16


def bits_of(near, far):
    chip = ((near >> 1) & 1, far & 1, (far >> 1) & 1)
    return ((near & 1) ^ chip[0] ^ chip[1] ^ chip[2],) + chip


def from_partner(values, *bit_of_role):
    nears, fars = lax.axis_size("near"), lax.axis_size("far")
    pairs = []
    for near in range(nears):
        for far in range(fars):
            bit = bit_of_role[bits_of(near, far)[0]]
            to_near = near ^ 1 ^ (2 if bit == 1 else 0)
            to_far = far ^ (1 << (bit - 2)) if bit >= 2 else far
            pairs.append((near * fars + far, to_near * fars + to_far))
    return lax.ppermute(values, ("near", "far"), pairs)


def split(values, bit):
    rows = values.shape[0] // 2
    low, high = values[:rows], values[rows:]
    return jnp.where(bit == 0, low, high), jnp.where(bit == 0, high, low)


def join(own, other, bit):
    return jnp.concatenate([jnp.where(bit == 0, own, other), jnp.where(bit == 0, other, own)])


def chain(total, order, bits):
    even, odd = order
    first = jnp.where(bits[0] == 0, bits[even[0]], bits[odd[0]])
    keep, send = split(total, first)
    own = keep + from_partner(send, even[0], odd[0])
    own = own + from_partner(own, even[1], odd[1])
    own = own + from_partner(own, even[2], odd[2])
    return join(own, from_partner(own, even[0], odd[0]), first)


def sum_over_cube(keep, send, orders, bits):
    total = keep + from_partner(send, 0, 0)
    rows = total.shape[0] // len(orders)
    parts = [chain(total[rows * k : rows * (k + 1)], order, bits) for k, order in enumerate(orders)]
    over = [from_partner(part, 0, 0) for part in parts]
    return join(jnp.concatenate(parts), jnp.concatenate(over), bits[0])


def halves(values):
    high = values.astype(bf16)
    return high, (values - high.astype(f32)).astype(bf16)


def product(left, right, contract):
    total = None
    for i, a in enumerate(left):
        for j, b in enumerate(right):
            if i + j < 2:
                term = lax.dot_general(a, b, (contract, ((), ())), preferred_element_type=f32)
                total = term if total is None else total + term
    return total


def parts_of(values):
    return (values,) if values.dtype == bf16 else halves(values)


NN = ((1,), (0,))
NT = ((1,), (1,))


def expand_kernel(first, role_ref, x_in, g_in, r_in, e_in, *refs):
    if first:
        keep_ref, send_ref, zh_ref, zl_ref, slope_ref, x_ref, r_ref, e_ref, g_ref, sems = refs
        copies = [
            pltpu.make_async_copy(source, target, sems.at[i])
            for i, (source, target) in enumerate(((r_in, r_ref), (x_in.at[0], x_ref), (e_in, e_ref), (g_in.at[0], g_ref)))
        ]
        for copy in copies:
            copy.start()
        copies[0].wait()
        copies[1].wait()
    else:
        keep_ref, send_ref, zh_ref, zl_ref, slope_ref = refs
        x_ref, g_ref, r_ref, e_ref = x_in, g_in, r_in, e_in
    width, columns = r_ref.shape
    reduce_scale = 1.0 / math.sqrt(columns)
    expand_scale = 1.0 / math.sqrt(width)
    feats = x_ref[...]
    pre = product(parts_of(r_ref[...]), (feats,), NT) * reduce_scale
    sig = jax.nn.sigmoid(pre)
    hidden = pre * sig
    slope_ref[...] = sig * (1.0 + pre * (1.0 - sig))
    hidden_t = halves(hidden)
    hidden_n = halves(hidden.T)
    if first:
        copies[2].wait()
    e_parts = parts_of(e_ref[...])
    summed = feats.astype(f32) + product(hidden_n, e_parts, NN) * expand_scale
    if first:
        copies[3].wait()
    sig = jax.nn.sigmoid(summed)
    grads = halves(g_ref[...].astype(f32) * (sig * (1.0 + summed * (1.0 - sig))))
    zh_ref[...] = grads[0]
    zl_ref[...] = grads[1]
    stepped = (e_ref[...].astype(f32) - learn_rate * expand_scale * product(hidden_t, grads, NN)) * (0.5**BITS)
    rows = width // 2
    even = role_ref[0] == 0
    keep_ref[...] = jnp.where(even, stepped[:rows], stepped[rows:])
    send_ref[...] = jnp.where(even, stepped[rows:], stepped[:rows])


def reduce_kernel(upcoming, role_ref, x_all, g_all, x_ref, r_ref, e_ref, zh_ref, zl_ref, slope_ref, keep_ref, send_ref, *refs):
    if upcoming is not None:
        next_x_ref, next_g_ref, sems = refs
        copies = (
            pltpu.make_async_copy(x_all.at[upcoming], next_x_ref, sems.at[0]),
            pltpu.make_async_copy(g_all.at[upcoming], next_g_ref, sems.at[1]),
        )
        for copy in copies:
            copy.start()
    width, columns = r_ref.shape
    reduce_scale = 1.0 / math.sqrt(columns)
    expand_scale = 1.0 / math.sqrt(width)
    grad_hidden = product(parts_of(e_ref[...]), (zh_ref[...], zl_ref[...]), NT) * expand_scale
    grad_pre = halves(grad_hidden * slope_ref[...])
    stepped = (r_ref[...].astype(f32) - learn_rate * reduce_scale * product(grad_pre, (x_ref[...],), NN)) * (0.5**BITS)
    rows = width // 2
    even = role_ref[0] == 0
    keep_ref[...] = jnp.where(even, stepped[:rows], stepped[rows:])
    send_ref[...] = jnp.where(even, stepped[rows:], stepped[:rows])
    if upcoming is not None:
        for copy in copies:
            copy.wait()


def shards(w_reduce, w_expand, inputs, out_grads):
    bits = bits_of(lax.axis_index("near"), lax.axis_index("far"))
    role = bits[0].astype(jnp.int32).reshape(1)
    held = [pltpu.with_memory_space_constraint(array[0, 0], pltpu.HBM) for array in (w_reduce, w_expand, inputs, out_grads)]
    reducing, expanding, inputs, out_grads = held
    iterations, rows, columns = inputs.shape
    width = reducing.shape[0]
    vmem = pl.BlockSpec(memory_space=pltpu.VMEM)
    smem = pl.BlockSpec(memory_space=pltpu.SMEM)
    hbm = pl.BlockSpec(memory_space=pltpu.HBM)
    half = jax.ShapeDtypeStruct((width // 2, columns), f32)
    acts = jax.ShapeDtypeStruct((rows, columns), bf16)
    weights = jax.ShapeDtypeStruct((width, columns), bf16)
    slopes = jax.ShapeDtypeStruct((width, rows), f32)
    params = pltpu.CompilerParams(vmem_limit_bytes=VMEM_LIMIT)
    feats = grads = None
    for iteration in range(iterations):
        first, last = iteration == 0, iteration == iterations - 1
        expand = pl.pallas_call(
            functools.partial(expand_kernel, first),
            out_shape=(half, half, acts, acts, slopes) + ((acts, weights, weights) if first else ()),
            in_specs=[smem] + [hbm if first else vmem] * 4,
            out_specs=(vmem,) * (8 if first else 5),
            scratch_shapes=[pltpu.VMEM((rows, columns), bf16), pltpu.SemaphoreType.DMA((4,))] if first else [],
            compiler_params=params,
            name=f"expand_{iteration}",
        )
        if first:
            keep_e, send_e, zh, zl, slope, feats, reducing, expanding = expand(role, inputs, out_grads, reducing, expanding)
        else:
            keep_e, send_e, zh, zl, slope = expand(role, feats, grads, reducing, expanding)
        results = pl.pallas_call(
            functools.partial(reduce_kernel, None if last else iteration + 1),
            out_shape=(half, half) + (() if last else (acts, acts)),
            in_specs=[smem, hbm, hbm] + [vmem] * 6,
            out_specs=(vmem,) * (2 if last else 4),
            scratch_shapes=[] if last else [pltpu.SemaphoreType.DMA((2,))],
            compiler_params=params,
            name=f"reduce_{iteration}",
        )(role, inputs, out_grads, feats, reducing, expanding, zh, zl, slope)
        keep_r, send_r = results[:2]
        if not last:
            feats, grads = results[2:]
        expanding = sum_over_cube(keep_e, send_e, ORDERS[:2], bits)
        reducing = sum_over_cube(keep_r, send_r, ORDERS[2:], bits)
    return (reducing[None, None], expanding[None, None])


def solution(mesh):
    in_specs = (
        P("near", "far", None, None),
        P("near", "far", None, None),
        P("near", "far", None, None, None),
        P("near", "far", None, None, None),
    )
    out_specs = (P("near", "far", None, None), P("near", "far", None, None))
    return jax.shard_map(shards, mesh=mesh, in_specs=in_specs, out_specs=out_specs, check_vma=False)
```

```python
import functools
import math

import jax
import jax.numpy as jnp
from jax import lax
from jax.experimental import pallas as pl
from jax.experimental.pallas import tpu as pltpu
from jax.sharding import PartitionSpec as P


learn_rate = 1.0

ORDERS = (
    ((1, 2, 3), (2, 3, 1)),
    ((3, 1, 2), (1, 2, 3)),
    ((2, 3, 1), (3, 1, 2)),
    ((1, 2, 3), (2, 3, 1)),
)
BITS = 4
SMEM = pl.BlockSpec(memory_space=pltpu.SMEM)
VMEM = pl.BlockSpec(memory_space=pltpu.VMEM)
HBM = pl.BlockSpec(memory_space=pltpu.HBM)
SMALL = pltpu.CompilerParams(vmem_limit_bytes=2**20)
LARGE = pltpu.CompilerParams(vmem_limit_bytes=12 * 2**20)
f32, bf16 = jnp.float32, jnp.bfloat16


def bits_of(near, far):
    chip = ((near >> 1) & 1, far & 1, (far >> 1) & 1)
    return ((near & 1) ^ chip[0] ^ chip[1] ^ chip[2],) + chip


def from_partner(values, *bit_of_role):
    nears, fars = lax.axis_size("near"), lax.axis_size("far")
    pairs = []
    for near in range(nears):
        for far in range(fars):
            bit = bit_of_role[bits_of(near, far)[0]]
            to_near = near ^ 1 ^ (2 if bit == 1 else 0)
            to_far = far ^ (1 << (bit - 2)) if bit >= 2 else far
            pairs.append((near * fars + far, to_near * fars + to_far))
    return lax.ppermute(values, ("near", "far"), pairs)


def join_kernel(index, places_ref, own_ref, rest_ref, out_ref):
    rows = own_ref.shape[0]
    place = places_ref[index]
    out_ref[pl.ds(pl.multiple_of(place * rows, rows), rows), :] = own_ref[...]
    out_ref[pl.ds(pl.multiple_of((1 - place) * rows, rows), rows), :] = rest_ref[...]


def chain(keep, send, index, places):
    even, odd = ORDERS[index - 1]
    own = keep + from_partner(send, even[0], odd[0])
    own = own + from_partner(own, even[1], odd[1])
    own = own + from_partner(own, even[2], odd[2])
    rest = from_partner(own, even[0], odd[0])
    rows, columns = own.shape
    return pl.pallas_call(
        functools.partial(join_kernel, index),
        out_shape=jax.ShapeDtypeStruct((2 * rows, columns), f32),
        in_specs=[SMEM, VMEM, VMEM],
        out_specs=VMEM,
        compiler_params=SMALL,
    )(places, own, rest)


def meet_kernel(indices, places_ref, keep_ref, got_ref, *outs):
    rows = outs[0].shape[0]
    for k, index in enumerate(indices):
        low, high = pl.ds(2 * k * rows, rows), pl.ds((2 * k + 1) * rows, rows)
        stays_low = places_ref[index] == 0
        low, high = keep_ref[low, :] + got_ref[low, :], keep_ref[high, :] + got_ref[high, :]
        outs[2 * k][...] = jnp.where(stays_low, low, high)
        outs[2 * k + 1][...] = jnp.where(stays_low, high, low)


def sum_over_cube(keep, send, indices, places):
    rows, columns = keep.shape
    count = 2 * len(indices)
    got = pltpu.with_memory_space_constraint(from_partner(send, 0, 0), pltpu.VMEM)
    pieces = pl.pallas_call(
        functools.partial(meet_kernel, indices),
        out_shape=(jax.ShapeDtypeStruct((rows // count, columns), f32),) * count,
        in_specs=[SMEM, VMEM, VMEM],
        out_specs=(VMEM,) * count,
        compiler_params=SMALL,
    )(places, keep, got)
    parts = [chain(pieces[2 * k], pieces[2 * k + 1], index, places) for k, index in enumerate(indices)]
    return parts + [from_partner(part, 0, 0) for part in parts]


def place_of(index, count, role):
    per_role = count // 2
    return (role if index < per_role else 1 - role) * per_role + index % per_role


def store_kernel(places_ref, *refs):
    *parts, out_ref, sems = refs
    rows = parts[0].shape[0]
    copies = []
    for i, part in enumerate(parts):
        start = pl.multiple_of(place_of(i, len(parts), places_ref[0]) * rows, rows)
        copies.append(pltpu.make_async_copy(part, out_ref.at[pl.ds(start, rows), :], sems.at[i]))
        copies[-1].start()
    for copy in copies:
        copy.wait()


def store(parts, places):
    rows, columns = parts[0].shape
    return pl.pallas_call(
        store_kernel,
        out_shape=jax.ShapeDtypeStruct((rows * len(parts), columns), f32),
        in_specs=[SMEM] + [VMEM] * len(parts),
        out_specs=HBM,
        scratch_shapes=[pltpu.SemaphoreType.DMA((len(parts),))],
        compiler_params=SMALL,
    )(places, *parts)


def halves(values):
    high = values.astype(bf16)
    return high, (values - high.astype(f32)).astype(bf16)


def product(left, right, contract):
    total = None
    for i, a in enumerate(left):
        for j, b in enumerate(right):
            if i + j < 2:
                term = lax.dot_general(a, b, (contract, ((), ())), preferred_element_type=f32)
                total = term if total is None else total + term
    return total


def parts_of(values):
    return (values,) if values.dtype == bf16 else halves(values)


NN = ((1,), (0,))
NT = ((1,), (1,))


def expand_kernel(count, places_ref, x_in, g_in, *refs):
    if count:
        r_parts, e_parts, outs = refs[:count], refs[count : 2 * count], refs[2 * count :]
        keep_ref, send_ref, zh_ref, zl_ref, slope_ref, r_ref, e_ref = outs
        x_ref, g_ref = x_in, g_in
        rows = r_parts[0].shape[0]
        for parts, whole_ref in ((r_parts, r_ref), (e_parts, e_ref)):
            for i, part in enumerate(parts):
                start = pl.multiple_of(place_of(i, count, places_ref[0]) * rows, rows)
                whole_ref[pl.ds(start, rows), :] = part[...]
    else:
        r_in, e_in, keep_ref, send_ref, zh_ref, zl_ref, slope_ref, r_ref, e_ref, x_ref, g_ref, sems = refs
        copies = [
            pltpu.make_async_copy(source, target, sems.at[i])
            for i, (source, target) in enumerate(((r_in, r_ref), (x_in.at[0], x_ref), (e_in, e_ref), (g_in.at[0], g_ref)))
        ]
        for copy in copies:
            copy.start()
        copies[0].wait()
        copies[1].wait()
    width, columns = r_ref.shape
    reduce_scale = 1.0 / math.sqrt(columns)
    expand_scale = 1.0 / math.sqrt(width)
    feats = x_ref[...]
    pre = product(parts_of(r_ref[...]), (feats,), NT) * reduce_scale
    sig = jax.nn.sigmoid(pre)
    hidden = pre * sig
    slope_ref[...] = sig * (1.0 + pre * (1.0 - sig))
    hidden_t = halves(hidden)
    hidden_n = halves(hidden.T)
    if not count:
        copies[2].wait()
    e_parts = parts_of(e_ref[...])
    summed = feats.astype(f32) + product(hidden_n, e_parts, NN) * expand_scale
    if not count:
        copies[3].wait()
    sig = jax.nn.sigmoid(summed)
    grads = halves(g_ref[...].astype(f32) * (sig * (1.0 + summed * (1.0 - sig))))
    zh_ref[...] = grads[0]
    zl_ref[...] = grads[1]
    stepped = (e_ref[...].astype(f32) - learn_rate * expand_scale * product(hidden_t, grads, NN)) * (0.5**BITS)
    rows = width // 2
    even = places_ref[0] == 0
    keep_ref[...] = jnp.where(even, stepped[:rows], stepped[rows:])
    send_ref[...] = jnp.where(even, stepped[rows:], stepped[:rows])


def reduce_kernel(upcoming, places_ref, x_all, g_all, x_ref, r_ref, e_ref, zh_ref, zl_ref, slope_ref, keep_ref, send_ref, *refs):
    if upcoming is not None:
        next_x_ref, next_g_ref, sems = refs
        copies = (
            pltpu.make_async_copy(x_all.at[upcoming], next_x_ref, sems.at[0]),
            pltpu.make_async_copy(g_all.at[upcoming], next_g_ref, sems.at[1]),
        )
        for copy in copies:
            copy.start()
    width, columns = r_ref.shape
    reduce_scale = 1.0 / math.sqrt(columns)
    expand_scale = 1.0 / math.sqrt(width)
    grad_hidden = product(parts_of(e_ref[...]), (zh_ref[...], zl_ref[...]), NT) * expand_scale
    grad_pre = halves(grad_hidden * slope_ref[...])
    stepped = (r_ref[...].astype(f32) - learn_rate * reduce_scale * product(grad_pre, (x_ref[...],), NN)) * (0.5**BITS)
    rows = width // 2
    even = places_ref[0] == 0
    keep_ref[...] = jnp.where(even, stepped[:rows], stepped[rows:])
    send_ref[...] = jnp.where(even, stepped[rows:], stepped[:rows])
    if upcoming is not None:
        for copy in copies:
            copy.wait()


def shards(w_reduce, w_expand, inputs, out_grads):
    bits = bits_of(lax.axis_index("near"), lax.axis_index("far"))
    places = jnp.stack([bits[0]] + [jnp.where(bits[0] == 0, bits[even[0]], bits[odd[0]]) for even, odd in ORDERS]).astype(jnp.int32)
    held = [pltpu.with_memory_space_constraint(array[0, 0], pltpu.HBM) for array in (w_reduce, w_expand, inputs, out_grads)]
    reducing, expanding, inputs, out_grads = held
    iterations, rows, columns = inputs.shape
    width = reducing.shape[0]
    half = jax.ShapeDtypeStruct((width // 2, columns), f32)
    acts = jax.ShapeDtypeStruct((rows, columns), bf16)
    slopes = jax.ShapeDtypeStruct((width, rows), f32)
    for iteration in range(iterations):
        first, last = iteration == 0, iteration == iterations - 1
        weights = jax.ShapeDtypeStruct((width, columns), bf16 if first else f32)
        results = pl.pallas_call(
            functools.partial(expand_kernel, 0 if first else len(sums_r)),
            out_shape=(half, half, acts, acts, slopes, weights, weights) + ((acts,) if first else ()),
            in_specs=[SMEM] + ([HBM] * 4 if first else [VMEM] * (2 + len(sums_r) + len(sums_e))),
            out_specs=(VMEM,) * (8 if first else 7),
            scratch_shapes=[pltpu.VMEM((rows, columns), bf16), pltpu.SemaphoreType.DMA((4,))] if first else [],
            compiler_params=LARGE,
        )(places, *((inputs, out_grads, reducing, expanding) if first else (feats, grads, *sums_r, *sums_e)))
        keep_e, send_e, zh, zl, slope, reducing, expanding = results[:7]
        if first:
            feats = results[7]
        results = pl.pallas_call(
            functools.partial(reduce_kernel, None if last else iteration + 1),
            out_shape=(half, half) + (() if last else (acts, acts)),
            in_specs=[SMEM, HBM, HBM] + [VMEM] * 6,
            out_specs=(VMEM,) * (2 if last else 4),
            scratch_shapes=[] if last else [pltpu.SemaphoreType.DMA((2,))],
            compiler_params=LARGE,
        )(places, inputs, out_grads, feats, reducing, expanding, zh, zl, slope)
        keep_r, send_r = results[:2]
        if not last:
            feats, grads = results[2:]
        sums_e = sum_over_cube(keep_e, send_e, (1, 2), places)
        sums_r = sum_over_cube(keep_r, send_r, (3, 4), places)
    return (store(sums_r, places)[None, None], store(sums_e, places)[None, None])


def solution(mesh):
    in_specs = (
        P("near", "far", None, None),
        P("near", "far", None, None),
        P("near", "far", None, None, None),
        P("near", "far", None, None, None),
    )
    out_specs = (P("near", "far", None, None), P("near", "far", None, None))
    return jax.shard_map(shards, mesh=mesh, in_specs=in_specs, out_specs=out_specs, check_vma=False)
```

```python
import functools
import math

import jax
import jax.numpy as jnp
from jax import lax
from jax.experimental import pallas as pl
from jax.experimental.pallas import tpu as pltpu
from jax.sharding import PartitionSpec as P


learn_rate = 1.0

ORDERS = (
    ((1, 2, 3), (2, 3, 1)),
    ((3, 1, 2), (1, 2, 3)),
    ((2, 3, 1), (3, 1, 2)),
    ((1, 2, 3), (2, 3, 1)),
)
BITS = 4
VMEM = pl.BlockSpec(memory_space=pltpu.VMEM)
HBM = pl.BlockSpec(memory_space=pltpu.HBM)
SMALL = pltpu.CompilerParams(vmem_limit_bytes=2**20)
LARGE = pltpu.CompilerParams(vmem_limit_bytes=12 * 2**20)
f32, bf16 = jnp.float32, jnp.bfloat16


def bits_of(near, far):
    chip = ((near >> 1) & 1, far & 1, (far >> 1) & 1)
    return ((near & 1) ^ chip[0] ^ chip[1] ^ chip[2],) + chip


def places():
    bits = bits_of(lax.axis_index("near"), lax.axis_index("far"))
    return [bits[0]] + [jnp.where(bits[0] == 0, bits[even[0]], bits[odd[0]]) for even, odd in ORDERS]


def from_partner(values, *bit_of_role):
    nears, fars = lax.axis_size("near"), lax.axis_size("far")
    pairs = []
    for near in range(nears):
        for far in range(fars):
            bit = bit_of_role[bits_of(near, far)[0]]
            to_near = near ^ 1 ^ (2 if bit == 1 else 0)
            to_far = far ^ (1 << (bit - 2)) if bit >= 2 else far
            pairs.append((near * fars + far, to_near * fars + to_far))
    return lax.ppermute(values, ("near", "far"), pairs)


def join_kernel(index, own_ref, rest_ref, out_ref):
    rows = own_ref.shape[0]
    place = places()[index]
    out_ref[pl.ds(pl.multiple_of(place * rows, rows), rows), :] = own_ref[...]
    out_ref[pl.ds(pl.multiple_of((1 - place) * rows, rows), rows), :] = rest_ref[...]


def chain(keep, send, index):
    even, odd = ORDERS[index - 1]
    own = keep + from_partner(send, even[0], odd[0])
    own = own + from_partner(own, even[1], odd[1])
    own = own + from_partner(own, even[2], odd[2])
    rest = from_partner(own, even[0], odd[0])
    rows, columns = own.shape
    return pl.pallas_call(
        functools.partial(join_kernel, index),
        out_shape=jax.ShapeDtypeStruct((2 * rows, columns), f32),
        in_specs=[VMEM, VMEM],
        out_specs=VMEM,
        compiler_params=SMALL,
    )(own, rest)


def meet_kernel(indices, keep_ref, got_ref, *outs):
    rows = outs[0].shape[0]
    place = places()
    for k, index in enumerate(indices):
        low, high = pl.ds(2 * k * rows, rows), pl.ds((2 * k + 1) * rows, rows)
        stays_low = place[index] == 0
        low, high = keep_ref[low, :] + got_ref[low, :], keep_ref[high, :] + got_ref[high, :]
        outs[2 * k][...] = jnp.where(stays_low, low, high)
        outs[2 * k + 1][...] = jnp.where(stays_low, high, low)


def sum_over_cube(keep, send, indices):
    rows, columns = keep.shape
    count = 2 * len(indices)
    got = pltpu.with_memory_space_constraint(from_partner(send, 0, 0), pltpu.VMEM)
    pieces = pl.pallas_call(
        functools.partial(meet_kernel, indices),
        out_shape=(jax.ShapeDtypeStruct((rows // count, columns), f32),) * count,
        in_specs=[VMEM, VMEM],
        out_specs=(VMEM,) * count,
        compiler_params=SMALL,
    )(keep, got)
    parts = [chain(pieces[2 * k], pieces[2 * k + 1], index) for k, index in enumerate(indices)]
    return parts + [from_partner(part, 0, 0) for part in parts]


def place_of(index, count, role):
    per_role = count // 2
    return (role if index < per_role else 1 - role) * per_role + index % per_role


def store_kernel(count, *refs):
    parts, outs, sems = refs[: 2 * count], refs[2 * count : -1], refs[-1]
    rows = parts[0].shape[0]
    role = places()[0]
    copies = []
    for i, part in enumerate(parts):
        start = pl.multiple_of(place_of(i % count, count, role) * rows, rows)
        copies.append(pltpu.make_async_copy(part, outs[i // count].at[pl.ds(start, rows), :], sems.at[i]))
        copies[-1].start()
    for copy in copies:
        copy.wait()


def store(reducing, expanding):
    rows, columns = reducing[0].shape
    count = len(reducing)
    return pl.pallas_call(
        functools.partial(store_kernel, count),
        out_shape=(jax.ShapeDtypeStruct((rows * count, columns), f32),) * 2,
        in_specs=[VMEM] * (2 * count),
        out_specs=(HBM, HBM),
        scratch_shapes=[pltpu.SemaphoreType.DMA((2 * count,))],
        compiler_params=SMALL,
        name="store",
    )(*reducing, *expanding)


def halves(values):
    high = values.astype(bf16)
    return high, (values - high.astype(f32)).astype(bf16)


def product(left, right, contract):
    total = None
    for i, a in enumerate(left):
        for j, b in enumerate(right):
            if i + j < 2:
                term = lax.dot_general(a, b, (contract, ((), ())), preferred_element_type=f32)
                total = term if total is None else total + term
    return total


def parts_of(values):
    return (values,) if values.dtype == bf16 else halves(values)


NN = ((1,), (0,))
NT = ((1,), (1,))


def expand_kernel(count, x_in, g_in, *refs):
    if count:
        r_parts, e_parts, outs = refs[:count], refs[count : 2 * count], refs[2 * count :]
        keep_ref, send_ref, zh_ref, zl_ref, slope_ref, r_ref, e_ref = outs
        x_ref, g_ref = x_in, g_in
        rows = r_parts[0].shape[0]
        role = places()[0]
        for parts, whole_ref in ((r_parts, r_ref), (e_parts, e_ref)):
            for i, part in enumerate(parts):
                start = pl.multiple_of(place_of(i, count, role) * rows, rows)
                whole_ref[pl.ds(start, rows), :] = part[...]
    else:
        r_in, e_in, keep_ref, send_ref, zh_ref, zl_ref, slope_ref, r_ref, e_ref, x_ref, g_ref, sems = refs
        copies = [
            pltpu.make_async_copy(source, target, sems.at[i])
            for i, (source, target) in enumerate(((r_in, r_ref), (x_in.at[0], x_ref), (e_in, e_ref), (g_in.at[0], g_ref)))
        ]
        for copy in copies:
            copy.start()
        copies[0].wait()
        copies[1].wait()
    width, columns = r_ref.shape
    reduce_scale = 1.0 / math.sqrt(columns)
    expand_scale = 1.0 / math.sqrt(width)
    feats = x_ref[...]
    pre = product(parts_of(r_ref[...]), (feats,), NT) * reduce_scale
    sig = jax.nn.sigmoid(pre)
    hidden = pre * sig
    slope_ref[...] = sig * (1.0 + pre * (1.0 - sig))
    hidden_t = halves(hidden)
    hidden_n = halves(hidden.T)
    if not count:
        copies[2].wait()
    e_parts = parts_of(e_ref[...])
    summed = feats.astype(f32) + product(hidden_n, e_parts, NN) * expand_scale
    if not count:
        copies[3].wait()
    sig = jax.nn.sigmoid(summed)
    grads = halves(g_ref[...].astype(f32) * (sig * (1.0 + summed * (1.0 - sig))))
    zh_ref[...] = grads[0]
    zl_ref[...] = grads[1]
    stepped = (e_ref[...].astype(f32) - learn_rate * expand_scale * product(hidden_t, grads, NN)) * (0.5**BITS)
    rows = width // 2
    even = places()[0] == 0
    keep_ref[...] = jnp.where(even, stepped[:rows], stepped[rows:])
    send_ref[...] = jnp.where(even, stepped[rows:], stepped[:rows])


def reduce_kernel(upcoming, x_all, g_all, x_ref, r_ref, e_ref, zh_ref, zl_ref, slope_ref, keep_ref, send_ref, *refs):
    if upcoming is not None:
        next_x_ref, next_g_ref, sems = refs
        copies = (
            pltpu.make_async_copy(x_all.at[upcoming], next_x_ref, sems.at[0]),
            pltpu.make_async_copy(g_all.at[upcoming], next_g_ref, sems.at[1]),
        )
        for copy in copies:
            copy.start()
    width, columns = r_ref.shape
    reduce_scale = 1.0 / math.sqrt(columns)
    expand_scale = 1.0 / math.sqrt(width)
    grad_hidden = product(parts_of(e_ref[...]), (zh_ref[...], zl_ref[...]), NT) * expand_scale
    grad_pre = halves(grad_hidden * slope_ref[...])
    stepped = (r_ref[...].astype(f32) - learn_rate * reduce_scale * product(grad_pre, (x_ref[...],), NN)) * (0.5**BITS)
    rows = width // 2
    even = places()[0] == 0
    keep_ref[...] = jnp.where(even, stepped[:rows], stepped[rows:])
    send_ref[...] = jnp.where(even, stepped[rows:], stepped[:rows])
    if upcoming is not None:
        for copy in copies:
            copy.wait()


def shards(w_reduce, w_expand, inputs, out_grads):
    held = [pltpu.with_memory_space_constraint(array[0, 0], pltpu.HBM) for array in (w_reduce, w_expand, inputs, out_grads)]
    reducing, expanding, inputs, out_grads = held
    iterations, rows, columns = inputs.shape
    width = reducing.shape[0]
    half = jax.ShapeDtypeStruct((width // 2, columns), f32)
    acts = jax.ShapeDtypeStruct((rows, columns), bf16)
    slopes = jax.ShapeDtypeStruct((width, rows), f32)
    for iteration in range(iterations):
        first, last = iteration == 0, iteration == iterations - 1
        weights = jax.ShapeDtypeStruct((width, columns), bf16 if first else f32)
        results = pl.pallas_call(
            functools.partial(expand_kernel, 0 if first else len(sums_r)),
            out_shape=(half, half, acts, acts, slopes, weights, weights) + ((acts,) if first else ()),
            in_specs=[HBM] * 4 if first else [VMEM] * (2 + len(sums_r) + len(sums_e)),
            out_specs=(VMEM,) * (8 if first else 7),
            scratch_shapes=[pltpu.VMEM((rows, columns), bf16), pltpu.SemaphoreType.DMA((4,))] if first else [],
            compiler_params=LARGE,
        )(*((inputs, out_grads, reducing, expanding) if first else (feats, grads, *sums_r, *sums_e)))
        keep_e, send_e, zh, zl, slope, reducing, expanding = results[:7]
        if first:
            feats = results[7]
        results = pl.pallas_call(
            functools.partial(reduce_kernel, None if last else iteration + 1),
            out_shape=(half, half) + (() if last else (acts, acts)),
            in_specs=[HBM, HBM] + [VMEM] * 6,
            out_specs=(VMEM,) * (2 if last else 4),
            scratch_shapes=[] if last else [pltpu.SemaphoreType.DMA((2,))],
            compiler_params=LARGE,
        )(inputs, out_grads, feats, reducing, expanding, zh, zl, slope)
        keep_r, send_r = results[:2]
        if not last:
            feats, grads = results[2:]
        sums_e = sum_over_cube(keep_e, send_e, (1, 2))
        sums_r = sum_over_cube(keep_r, send_r, (3, 4))
    reducing, expanding = store(sums_r, sums_e)
    return reducing[None, None], expanding[None, None]


def solution(mesh):
    in_specs = (
        P("near", "far", None, None),
        P("near", "far", None, None),
        P("near", "far", None, None, None),
        P("near", "far", None, None, None),
    )
    out_specs = (P("near", "far", None, None), P("near", "far", None, None))
    return jax.shard_map(shards, mesh=mesh, in_specs=in_specs, out_specs=out_specs, check_vma=False)
```

```python
import functools
import math

import jax
import jax.numpy as jnp
from jax import lax
from jax.experimental import pallas as pl
from jax.experimental.pallas import tpu as pltpu
from jax.sharding import PartitionSpec as P


learn_rate = 1.0

ORDERS = (
    ((1, 2, 3), (2, 3, 1)),
    ((3, 1, 2), (1, 2, 3)),
    ((2, 3, 1), (3, 1, 2)),
    ((1, 2, 3), (2, 3, 1)),
)
BITS = 4
VMEM = pl.BlockSpec(memory_space=pltpu.VMEM)
HBM = pl.BlockSpec(memory_space=pltpu.HBM)
SMALL = pltpu.CompilerParams(vmem_limit_bytes=2**20)
LARGE = pltpu.CompilerParams(vmem_limit_bytes=12 * 2**20)
f32, bf16 = jnp.float32, jnp.bfloat16


def bits_of(near, far):
    chip = ((near >> 1) & 1, far & 1, (far >> 1) & 1)
    return ((near & 1) ^ chip[0] ^ chip[1] ^ chip[2],) + chip


def places():
    bits = bits_of(lax.axis_index("near"), lax.axis_index("far"))
    return [bits[0]] + [jnp.where(bits[0] == 0, bits[even[0]], bits[odd[0]]) for even, odd in ORDERS]


def from_partner(values, *bit_of_role):
    nears, fars = lax.axis_size("near"), lax.axis_size("far")
    pairs = []
    for near in range(nears):
        for far in range(fars):
            bit = bit_of_role[bits_of(near, far)[0]]
            to_near = near ^ 1 ^ (2 if bit == 1 else 0)
            to_far = far ^ (1 << (bit - 2)) if bit >= 2 else far
            pairs.append((near * fars + far, to_near * fars + to_far))
    return lax.ppermute(values, ("near", "far"), pairs)


def join_kernel(index, own_ref, rest_ref, out_ref):
    rows = own_ref.shape[0]
    place = places()[index]
    out_ref[pl.ds(pl.multiple_of(place * rows, rows), rows), :] = own_ref[...]
    out_ref[pl.ds(pl.multiple_of((1 - place) * rows, rows), rows), :] = rest_ref[...]


def chain(keep, send, index):
    even, odd = ORDERS[index - 1]
    got = from_partner(send, even[0], odd[0])
    own = keep + got
    own = own + from_partner(own, even[1], odd[1])
    own = own + from_partner(own, even[2], odd[2])
    rest = from_partner(own, even[0], odd[0])
    rows, columns = own.shape
    return pl.pallas_call(
        functools.partial(join_kernel, index),
        out_shape=jax.ShapeDtypeStruct((2 * rows, columns), f32),
        in_specs=[VMEM, VMEM],
        out_specs=VMEM,
        compiler_params=SMALL,
    )(own, rest)


def meet_kernel(indices, keep_ref, got_ref, *outs):
    rows = outs[0].shape[0]
    place = places()
    for k, index in enumerate(indices):
        low, high = pl.ds(2 * k * rows, rows), pl.ds((2 * k + 1) * rows, rows)
        stays_low = place[index] == 0
        low, high = keep_ref[low, :] + got_ref[low, :], keep_ref[high, :] + got_ref[high, :]
        outs[2 * k][...] = jnp.where(stays_low, low, high)
        outs[2 * k + 1][...] = jnp.where(stays_low, high, low)


def sum_over_cube(keep, send, indices):
    rows, columns = keep.shape
    count = 2 * len(indices)
    got = pltpu.with_memory_space_constraint(from_partner(send, 0, 0), pltpu.VMEM)
    pieces = pl.pallas_call(
        functools.partial(meet_kernel, indices),
        out_shape=(jax.ShapeDtypeStruct((rows // count, columns), f32),) * count,
        in_specs=[VMEM, VMEM],
        out_specs=(VMEM,) * count,
        compiler_params=SMALL,
    )(keep, got)
    parts = [chain(pieces[2 * k], pieces[2 * k + 1], index) for k, index in enumerate(indices)]
    return parts + [from_partner(part, 0, 0) for part in parts]


def place_of(index, count, role):
    per_role = count // 2
    return (role if index < per_role else 1 - role) * per_role + index % per_role


def store_kernel(count, *refs):
    parts, outs, sems = refs[: 2 * count], refs[2 * count : -1], refs[-1]
    rows = parts[0].shape[0]
    role = places()[0]
    copies = []
    for i, part in enumerate(parts):
        start = pl.multiple_of(place_of(i % count, count, role) * rows, rows)
        copies.append(pltpu.make_async_copy(part, outs[i // count].at[pl.ds(start, rows), :], sems.at[i]))
        copies[-1].start()
    for copy in copies:
        copy.wait()


def store(reducing, expanding):
    rows, columns = reducing[0].shape
    count = len(reducing)
    return pl.pallas_call(
        functools.partial(store_kernel, count),
        out_shape=(jax.ShapeDtypeStruct((rows * count, columns), f32),) * 2,
        in_specs=[VMEM] * (2 * count),
        out_specs=(HBM, HBM),
        scratch_shapes=[pltpu.SemaphoreType.DMA((2 * count,))],
        compiler_params=SMALL,
        name="store",
    )(*reducing, *expanding)


def halves(values):
    high = values.astype(bf16)
    return high, (values - high.astype(f32)).astype(bf16)


def product(left, right, contract):
    total = None
    for i, a in enumerate(left):
        for j, b in enumerate(right):
            if i + j < 2:
                term = lax.dot_general(a, b, (contract, ((), ())), preferred_element_type=f32)
                total = term if total is None else total + term
    return total


def parts_of(values):
    return (values,) if values.dtype == bf16 else halves(values)


NN = ((1,), (0,))
NT = ((1,), (1,))


def expand_kernel(count, x_in, g_in, *refs):
    if count:
        r_parts, e_parts, outs = refs[:count], refs[count : 2 * count], refs[2 * count :]
        keep_ref, send_ref, zh_ref, zl_ref, slope_ref, r_ref, e_ref = outs
        x_ref, g_ref = x_in, g_in
        rows = r_parts[0].shape[0]
        role = places()[0]
        for parts, whole_ref in ((r_parts, r_ref), (e_parts, e_ref)):
            for i, part in enumerate(parts):
                start = pl.multiple_of(place_of(i, count, role) * rows, rows)
                whole_ref[pl.ds(start, rows), :] = part[...]
    else:
        r_in, e_in, keep_ref, send_ref, zh_ref, zl_ref, slope_ref, r_ref, e_ref, x_ref, *later, g_ref, sems = refs
        moves = [(r_in, r_ref), (x_in.at[0], x_ref), (e_in, e_ref), (g_in.at[0], g_ref)]
        moves += [(source.at[1 + i // 2], ref) for i, (source, ref) in enumerate(zip((x_in, g_in) * len(later), later))]
        copies = [pltpu.make_async_copy(source, target, sems.at[i]) for i, (source, target) in enumerate(moves)]
        for copy in copies:
            copy.start()
        copies[0].wait()
        copies[1].wait()
    width, columns = r_ref.shape
    reduce_scale = 1.0 / math.sqrt(columns)
    expand_scale = 1.0 / math.sqrt(width)
    feats = x_ref[...]
    pre = product(parts_of(r_ref[...]), (feats,), NT) * reduce_scale
    sig = jax.nn.sigmoid(pre)
    hidden = pre * sig
    slope_ref[...] = sig * (1.0 + pre * (1.0 - sig))
    hidden_t = halves(hidden)
    hidden_n = halves(hidden.T)
    if not count:
        copies[2].wait()
    e_parts = parts_of(e_ref[...])
    summed = feats.astype(f32) + product(hidden_n, e_parts, NN) * expand_scale
    if not count:
        copies[3].wait()
    sig = jax.nn.sigmoid(summed)
    grads = halves(g_ref[...].astype(f32) * (sig * (1.0 + summed * (1.0 - sig))))
    zh_ref[...] = grads[0]
    zl_ref[...] = grads[1]
    stepped = (e_ref[...].astype(f32) - learn_rate * expand_scale * product(hidden_t, grads, NN)) * (0.5**BITS)
    rows = width // 2
    even = places()[0] == 0
    keep_ref[...] = jnp.where(even, stepped[:rows], stepped[rows:])
    send_ref[...] = jnp.where(even, stepped[rows:], stepped[:rows])
    if not count:
        for copy in copies[4:]:
            copy.wait()


def reduce_kernel(x_ref, r_ref, e_ref, zh_ref, zl_ref, slope_ref, keep_ref, send_ref):
    width, columns = r_ref.shape
    reduce_scale = 1.0 / math.sqrt(columns)
    expand_scale = 1.0 / math.sqrt(width)
    grad_hidden = product(parts_of(e_ref[...]), (zh_ref[...], zl_ref[...]), NT) * expand_scale
    grad_pre = halves(grad_hidden * slope_ref[...])
    stepped = (r_ref[...].astype(f32) - learn_rate * reduce_scale * product(grad_pre, (x_ref[...],), NN)) * (0.5**BITS)
    rows = width // 2
    even = places()[0] == 0
    keep_ref[...] = jnp.where(even, stepped[:rows], stepped[rows:])
    send_ref[...] = jnp.where(even, stepped[rows:], stepped[:rows])


def shards(w_reduce, w_expand, inputs, out_grads):
    held = [pltpu.with_memory_space_constraint(array[0, 0], pltpu.HBM) for array in (w_reduce, w_expand, inputs, out_grads)]
    reducing, expanding, inputs, out_grads = held
    iterations, rows, columns = inputs.shape
    width = reducing.shape[0]
    half = jax.ShapeDtypeStruct((width // 2, columns), f32)
    acts = jax.ShapeDtypeStruct((rows, columns), bf16)
    slopes = jax.ShapeDtypeStruct((width, rows), f32)
    for iteration in range(iterations):
        first = iteration == 0
        weights = jax.ShapeDtypeStruct((width, columns), bf16 if first else f32)
        results = pl.pallas_call(
            functools.partial(expand_kernel, 0 if first else len(sums_r)),
            out_shape=(half, half, acts, acts, slopes, weights, weights) + ((acts,) * (2 * iterations - 1) if first else ()),
            in_specs=[HBM] * 4 if first else [VMEM] * (2 + len(sums_r) + len(sums_e)),
            out_specs=(VMEM,) * (7 + (2 * iterations - 1 if first else 0)),
            scratch_shapes=[pltpu.VMEM((rows, columns), bf16), pltpu.SemaphoreType.DMA((2 * iterations + 2,))] if first else [],
            compiler_params=LARGE,
        )(*((inputs, out_grads, reducing, expanding) if first else (feats[iteration], grads[iteration], *sums_r, *sums_e)))
        keep_e, send_e, zh, zl, slope, reducing, expanding = results[:7]
        if first:
            feats, grads = (results[7], *results[8::2]), (None, *results[9::2])
        keep_r, send_r = pl.pallas_call(
            reduce_kernel, out_shape=(half, half), in_specs=[VMEM] * 6, out_specs=(VMEM,) * 2, compiler_params=LARGE
        )(feats[iteration], reducing, expanding, zh, zl, slope)
        sums_e = sum_over_cube(keep_e, send_e, (1, 2))
        sums_r = sum_over_cube(keep_r, send_r, (3, 4))
    reducing, expanding = store(sums_r, sums_e)
    return reducing[None, None], expanding[None, None]


def solution(mesh):
    in_specs = (
        P("near", "far", None, None),
        P("near", "far", None, None),
        P("near", "far", None, None, None),
        P("near", "far", None, None, None),
    )
    out_specs = (P("near", "far", None, None), P("near", "far", None, None))
    return jax.shard_map(shards, mesh=mesh, in_specs=in_specs, out_specs=out_specs, check_vma=False)
```

```python
import functools
import math

import jax
import jax.numpy as jnp
from jax import lax
from jax.experimental import pallas as pl
from jax.experimental.pallas import tpu as pltpu
from jax.sharding import PartitionSpec as P


learn_rate = 1.0

ORDERS = (
    ((1, 2, 3), (2, 3, 1)),
    ((3, 1, 2), (1, 2, 3)),
    ((2, 3, 1), (3, 1, 2)),
    ((1, 2, 3), (2, 3, 1)),
)
BITS = 4
VMEM = pl.BlockSpec(memory_space=pltpu.VMEM)
HBM = pl.BlockSpec(memory_space=pltpu.HBM)
SMALL = pltpu.CompilerParams(vmem_limit_bytes=2**20)
LARGE = pltpu.CompilerParams(vmem_limit_bytes=12 * 2**20)
f32, bf16 = jnp.float32, jnp.bfloat16


def bits_of(near, far):
    chip = ((near >> 1) & 1, far & 1, (far >> 1) & 1)
    return ((near & 1) ^ chip[0] ^ chip[1] ^ chip[2],) + chip


def places():
    bits = bits_of(lax.axis_index("near"), lax.axis_index("far"))
    return [bits[0]] + [jnp.where(bits[0] == 0, bits[even[0]], bits[odd[0]]) for even, odd in ORDERS]


def from_partner(values, *bit_of_role):
    nears, fars = lax.axis_size("near"), lax.axis_size("far")
    pairs = []
    for near in range(nears):
        for far in range(fars):
            bit = bit_of_role[bits_of(near, far)[0]]
            to_near = near ^ 1 ^ (2 if bit == 1 else 0)
            to_far = far ^ (1 << (bit - 2)) if bit >= 2 else far
            pairs.append((near * fars + far, to_near * fars + to_far))
    return lax.ppermute(values, ("near", "far"), pairs)


def join_kernel(index, own_ref, rest_ref, out_ref):
    rows = own_ref.shape[0]
    place = places()[index]
    out_ref[pl.ds(pl.multiple_of(place * rows, rows), rows), :] = own_ref[...]
    out_ref[pl.ds(pl.multiple_of((1 - place) * rows, rows), rows), :] = rest_ref[...]


def chain(keep, send, index):
    even, odd = ORDERS[index - 1]

    def exchanged(values, step):
        return from_partner(values, even[step % 3], odd[step % 3])

    own = keep + exchanged(send, 0)
    own = own + exchanged(own, 1)
    own = own + exchanged(own, 2)
    rest = exchanged(own, 3)
    rows, columns = own.shape
    joined = pl.pallas_call(
        functools.partial(join_kernel, index),
        out_shape=jax.ShapeDtypeStruct((2 * rows, columns), f32),
        in_specs=[VMEM, VMEM],
        out_specs=VMEM,
        compiler_params=SMALL,
    )(own, rest)
    return joined, from_partner(joined, 0, 0)


def meet_kernel(indices, keep_ref, got_ref, *outs):
    rows = outs[0].shape[0]
    place = places()
    for k, index in enumerate(indices):
        low, high = pl.ds(2 * k * rows, rows), pl.ds((2 * k + 1) * rows, rows)
        stays_low = place[index] == 0
        low, high = keep_ref[low, :] + got_ref[low, :], keep_ref[high, :] + got_ref[high, :]
        outs[2 * k][...] = jnp.where(stays_low, low, high)
        outs[2 * k + 1][...] = jnp.where(stays_low, high, low)


def sum_over_cube(keep, send, indices):
    rows, columns = keep.shape
    count = 2 * len(indices)
    got = pltpu.with_memory_space_constraint(from_partner(send, 0, 0), pltpu.VMEM)
    pieces = pl.pallas_call(
        functools.partial(meet_kernel, indices),
        out_shape=(jax.ShapeDtypeStruct((rows // count, columns), f32),) * count,
        in_specs=[VMEM, VMEM],
        out_specs=(VMEM,) * count,
        compiler_params=SMALL,
    )(keep, got)
    parts = [chain(pieces[2 * k], pieces[2 * k + 1], index) for k, index in enumerate(indices)]
    return [own for own, over in parts] + [over for own, over in parts]


def place_of(index, count, role):
    per_role = count // 2
    return (role if index < per_role else 1 - role) * per_role + index % per_role


def store_kernel(count, *refs):
    parts, outs, sems = refs[: 2 * count], refs[2 * count : -1], refs[-1]
    rows = parts[0].shape[0]
    role = places()[0]
    copies = []
    for i, part in enumerate(parts):
        start = pl.multiple_of(place_of(i % count, count, role) * rows, rows)
        copies.append(pltpu.make_async_copy(part, outs[i // count].at[pl.ds(start, rows), :], sems.at[i]))
        copies[-1].start()
    for copy in copies:
        copy.wait()


def store(reducing, expanding):
    rows, columns = reducing[0].shape
    count = len(reducing)
    return pl.pallas_call(
        functools.partial(store_kernel, count),
        out_shape=(jax.ShapeDtypeStruct((rows * count, columns), f32),) * 2,
        in_specs=[VMEM] * (2 * count),
        out_specs=(HBM, HBM),
        scratch_shapes=[pltpu.SemaphoreType.DMA((2 * count,))],
        compiler_params=SMALL,
        name="store",
    )(*reducing, *expanding)


def halves(values):
    high = values.astype(bf16)
    return high, (values - high.astype(f32)).astype(bf16)


def product(left, right, contract):
    total = None
    for i, a in enumerate(left):
        for j, b in enumerate(right):
            if i + j < 2:
                term = lax.dot_general(a, b, (contract, ((), ())), preferred_element_type=f32)
                total = term if total is None else total + term
    return total


def parts_of(values):
    return (values,) if values.dtype == bf16 else halves(values)


NN = ((1,), (0,))
NT = ((1,), (1,))


def expand_kernel(count, x_in, g_in, *refs):
    if count:
        r_parts, e_parts, outs = refs[:count], refs[count : 2 * count], refs[2 * count :]
        keep_ref, send_ref, zh_ref, zl_ref, slope_ref, r_ref, e_ref = outs
        x_ref, g_ref = x_in, g_in
        rows = r_parts[0].shape[0]
        role = places()[0]
        for parts, whole_ref in ((r_parts, r_ref), (e_parts, e_ref)):
            for i, part in enumerate(parts):
                start = pl.multiple_of(place_of(i, count, role) * rows, rows)
                whole_ref[pl.ds(start, rows), :] = part[...]
    else:
        r_in, e_in, keep_ref, send_ref, zh_ref, zl_ref, slope_ref, r_ref, e_ref, x_ref, *later, g_ref, sems = refs
        moves = [(r_in, r_ref), (x_in.at[0], x_ref), (e_in, e_ref), (g_in.at[0], g_ref)]
        moves += [(source.at[1 + i // 2], ref) for i, (source, ref) in enumerate(zip((x_in, g_in) * len(later), later))]
        copies = [pltpu.make_async_copy(source, target, sems.at[i]) for i, (source, target) in enumerate(moves)]
        for copy in copies:
            copy.start()
        copies[0].wait()
        copies[1].wait()
    width, columns = r_ref.shape
    reduce_scale = 1.0 / math.sqrt(columns)
    expand_scale = 1.0 / math.sqrt(width)
    feats = x_ref[...]
    pre = product(parts_of(r_ref[...]), (feats,), NT) * reduce_scale
    sig = jax.nn.sigmoid(pre)
    hidden = pre * sig
    slope_ref[...] = sig * (1.0 + pre * (1.0 - sig))
    hidden_t = halves(hidden)
    hidden_n = halves(hidden.T)
    if not count:
        copies[2].wait()
    e_parts = parts_of(e_ref[...])
    summed = feats.astype(f32) + product(hidden_n, e_parts, NN) * expand_scale
    if not count:
        copies[3].wait()
    sig = jax.nn.sigmoid(summed)
    grads = halves(g_ref[...].astype(f32) * (sig * (1.0 + summed * (1.0 - sig))))
    zh_ref[...] = grads[0]
    zl_ref[...] = grads[1]
    stepped = (e_ref[...].astype(f32) - learn_rate * expand_scale * product(hidden_t, grads, NN)) * (0.5**BITS)
    rows = width // 2
    even = places()[0] == 0
    keep_ref[...] = jnp.where(even, stepped[:rows], stepped[rows:])
    send_ref[...] = jnp.where(even, stepped[rows:], stepped[:rows])
    if not count:
        for copy in copies[4:]:
            copy.wait()


def reduce_kernel(x_ref, r_ref, e_ref, zh_ref, zl_ref, slope_ref, keep_ref, send_ref):
    width, columns = r_ref.shape
    reduce_scale = 1.0 / math.sqrt(columns)
    expand_scale = 1.0 / math.sqrt(width)
    grad_hidden = product(parts_of(e_ref[...]), (zh_ref[...], zl_ref[...]), NT) * expand_scale
    grad_pre = halves(grad_hidden * slope_ref[...])
    stepped = (r_ref[...].astype(f32) - learn_rate * reduce_scale * product(grad_pre, (x_ref[...],), NN)) * (0.5**BITS)
    rows = width // 2
    even = places()[0] == 0
    keep_ref[...] = jnp.where(even, stepped[:rows], stepped[rows:])
    send_ref[...] = jnp.where(even, stepped[rows:], stepped[:rows])


def shards(w_reduce, w_expand, inputs, out_grads):
    held = [pltpu.with_memory_space_constraint(array[0, 0], pltpu.HBM) for array in (w_reduce, w_expand, inputs, out_grads)]
    reducing, expanding, inputs, out_grads = held
    iterations, rows, columns = inputs.shape
    width = reducing.shape[0]
    half = jax.ShapeDtypeStruct((width // 2, columns), f32)
    acts = jax.ShapeDtypeStruct((rows, columns), bf16)
    slopes = jax.ShapeDtypeStruct((width, rows), f32)
    for iteration in range(iterations):
        first = iteration == 0
        weights = jax.ShapeDtypeStruct((width, columns), bf16 if first else f32)
        results = pl.pallas_call(
            functools.partial(expand_kernel, 0 if first else len(sums_r)),
            out_shape=(half, half, acts, acts, slopes, weights, weights) + ((acts,) * (2 * iterations - 1) if first else ()),
            in_specs=[HBM] * 4 if first else [VMEM] * (2 + len(sums_r) + len(sums_e)),
            out_specs=(VMEM,) * (7 + (2 * iterations - 1 if first else 0)),
            scratch_shapes=[pltpu.VMEM((rows, columns), bf16), pltpu.SemaphoreType.DMA((2 * iterations + 2,))] if first else [],
            compiler_params=LARGE,
        )(*((inputs, out_grads, reducing, expanding) if first else (feats[iteration], grads[iteration], *sums_r, *sums_e)))
        keep_e, send_e, zh, zl, slope, reducing, expanding = results[:7]
        if first:
            feats, grads = (results[7], *results[8::2]), (None, *results[9::2])
        keep_r, send_r = pl.pallas_call(
            reduce_kernel, out_shape=(half, half), in_specs=[VMEM] * 6, out_specs=(VMEM,) * 2, compiler_params=LARGE
        )(feats[iteration], reducing, expanding, zh, zl, slope)
        sums_e = sum_over_cube(keep_e, send_e, (1, 2))
        sums_r = sum_over_cube(keep_r, send_r, (3, 4))
    reducing, expanding = store(sums_r, sums_e)
    return reducing[None, None], expanding[None, None]


def solution(mesh):
    in_specs = (
        P("near", "far", None, None),
        P("near", "far", None, None),
        P("near", "far", None, None, None),
        P("near", "far", None, None, None),
    )
    out_specs = (P("near", "far", None, None), P("near", "far", None, None))
    return jax.shard_map(shards, mesh=mesh, in_specs=in_specs, out_specs=out_specs, check_vma=False)
```

```python
import functools
import math

import jax
import jax.numpy as jnp
from jax import lax
from jax.experimental import pallas as pl
from jax.experimental.pallas import tpu as pltpu
from jax.sharding import PartitionSpec as P


learn_rate = 1.0

ORDERS = (
    ((1, 3, 2), (3, 2, 1)),
    ((3, 2, 1), (2, 1, 3)),
    ((1, 3, 2), (2, 1, 3)),
    ((1, 3, 2), (3, 2, 1)),
)
EXPAND_CHAINS = ((1, 4), (2, 4))
REDUCE_CHAINS = ((3, 4), (4, 4))
BITS = 4
BLOCK = 256
VMEM = pl.BlockSpec(memory_space=pltpu.VMEM)
HBM = pl.BlockSpec(memory_space=pltpu.HBM)
SMALL = pltpu.CompilerParams(vmem_limit_bytes=2**20)
LARGE = pltpu.CompilerParams(vmem_limit_bytes=12 * 2**20)
f32, bf16 = jnp.float32, jnp.bfloat16


def bits_of(near, far):
    chip = ((near >> 1) & 1, far & 1, (far >> 1) & 1)
    return ((near & 1) ^ chip[0] ^ chip[1] ^ chip[2],) + chip


def places():
    bits = bits_of(lax.axis_index("near"), lax.axis_index("far"))
    return [bits[0]] + [jnp.where(bits[0] == 0, bits[even[0]], bits[odd[0]]) for even, odd in ORDERS]


def from_partner(values, *bit_of_role):
    nears, fars = lax.axis_size("near"), lax.axis_size("far")
    pairs = []
    for near in range(nears):
        for far in range(fars):
            bit = bit_of_role[bits_of(near, far)[0]]
            to_near = near ^ 1 ^ (2 if bit == 1 else 0)
            to_far = far ^ (1 << (bit - 2)) if bit >= 2 else far
            pairs.append((near * fars + far, to_near * fars + to_far))
    return lax.ppermute(values, ("near", "far"), pairs)


def join_kernel(index, own_ref, rest_ref, out_ref):
    rows = own_ref.shape[0]
    place = places()[index]
    out_ref[pl.ds(pl.multiple_of(place * rows, rows), rows), :] = own_ref[...]
    out_ref[pl.ds(pl.multiple_of((1 - place) * rows, rows), rows), :] = rest_ref[...]


def chain(keep, send, index):
    even, odd = ORDERS[index - 1]

    def exchanged(values, step):
        return from_partner(values, even[step % 3], odd[step % 3])

    own = keep + exchanged(send, 0)
    own = own + exchanged(own, 1)
    own = own + exchanged(own, 2)
    rest = exchanged(own, 3)
    rows, columns = own.shape
    joined = pl.pallas_call(
        functools.partial(join_kernel, index),
        out_shape=jax.ShapeDtypeStruct((2 * rows, columns), f32),
        in_specs=[VMEM, VMEM],
        out_specs=VMEM,
        compiler_params=SMALL,
    )(own, rest)
    return joined, from_partner(joined, 0, 0)


def spans(chains, rows):
    first = 0
    for index, eighths in chains:
        yield index, first, rows * eighths // 8
        first += rows * eighths // 8


def meet_kernel(chains, keep_ref, got_ref, *outs):
    place = places()
    for k, (index, first, rows) in enumerate(spans(chains, keep_ref.shape[0])):
        low, high = pl.ds(first, rows // 2), pl.ds(first + rows // 2, rows // 2)
        stays_low = place[index] == 0
        low, high = keep_ref[low, :] + got_ref[low, :], keep_ref[high, :] + got_ref[high, :]
        outs[2 * k][...] = jnp.where(stays_low, low, high)
        outs[2 * k + 1][...] = jnp.where(stays_low, high, low)


def sum_over_cube(keep, send, chains):
    rows, columns = keep.shape
    counts = [count // 2 for _, _, count in spans(chains, rows) for _ in range(2)]
    got = pltpu.with_memory_space_constraint(from_partner(send, 0, 0), pltpu.VMEM)
    pieces = pl.pallas_call(
        functools.partial(meet_kernel, chains),
        out_shape=[jax.ShapeDtypeStruct((count, columns), f32) for count in counts],
        in_specs=[VMEM, VMEM],
        out_specs=[VMEM] * len(counts),
        compiler_params=SMALL,
    )(keep, got)
    parts = [chain(pieces[2 * k], pieces[2 * k + 1], index) for k, (index, _) in enumerate(chains)]
    return [own for own, over in parts] + [over for own, over in parts]


def placed(parts, chains, role):
    rows = sum(part.shape[0] for part in parts) // 2
    firsts = [first for _, first, _ in spans(chains, rows)]
    for i, part in enumerate(parts):
        place = role if i < len(chains) else 1 - role
        yield part, pl.ds(pl.multiple_of(place * rows + firsts[i % len(chains)], 16), part.shape[0])


def store_kernel(*refs):
    *parts, reduce_ref, expand_ref, sems = refs
    role = places()[0]
    count = 2 * len(REDUCE_CHAINS)
    moves = [(part, reduce_ref.at[rows, :]) for part, rows in placed(parts[:count], REDUCE_CHAINS, role)]
    moves += [(part, expand_ref.at[rows, :]) for part, rows in placed(parts[count:], EXPAND_CHAINS, role)]
    copies = [pltpu.make_async_copy(source, target, sems.at[i]) for i, (source, target) in enumerate(moves)]
    for copy in copies:
        copy.start()
    for copy in copies:
        copy.wait()


def store(reducing, expanding):
    columns = reducing[0].shape[1]
    parts = [*reducing, *expanding]
    return pl.pallas_call(
        store_kernel,
        out_shape=[jax.ShapeDtypeStruct((sum(part.shape[0] for part in group), columns), f32) for group in (reducing, expanding)],
        in_specs=[VMEM] * len(parts),
        out_specs=[HBM, HBM],
        scratch_shapes=[pltpu.SemaphoreType.DMA((len(parts),))],
        compiler_params=SMALL,
        name="store",
    )(*parts)


def halves(values):
    high = values.astype(bf16)
    return high, (values - high.astype(f32)).astype(bf16)


def product(left, right, contract):
    total = None
    for i, a in enumerate(left):
        for j, b in enumerate(right):
            if i + j < 2:
                term = lax.dot_general(a, b, (contract, ((), ())), preferred_element_type=f32)
                total = term if total is None else total + term
    return total


def parts_of(values):
    return (values,) if values.dtype == bf16 else halves(values)


NN = ((1,), (0,))
NT = ((1,), (1,))


def in_columns(columns):
    return [pl.ds(start, BLOCK) for start in range(0, columns, BLOCK)]


def store_by_role(role, values, *refs):
    rows = values[0].shape[0] // 2
    for part, ref in zip(values, refs):
        ref[pl.ds(pl.multiple_of(role * rows, rows), rows), :] = part[:rows]
        ref[pl.ds(pl.multiple_of((1 - role) * rows, rows), rows), :] = part[rows:]


def step_columns(role, columns, weights_ref, step, keep_ref, send_ref):
    rows = keep_ref.shape[0]
    for i, (place, ref) in enumerate(((role, keep_ref), (1 - role, send_ref))):
        old = weights_ref[pl.ds(pl.multiple_of(place * rows, rows), rows), columns].astype(f32)
        ref[:, columns] = (old - step[i * rows : (i + 1) * rows]) * (0.5**BITS)


def expand_kernel(joined, x_in, g_in, *refs):
    role = places()[0]
    *refs, hidden_high_ref, hidden_low_ref = refs
    if joined:
        r_count, e_count = 2 * len(REDUCE_CHAINS), 2 * len(EXPAND_CHAINS)
        r_parts, e_parts, outs = refs[:r_count], refs[r_count : r_count + e_count], refs[r_count + e_count :]
        keep_ref, send_ref, zh_ref, zl_ref, slope_ref, r_ref, e_ref = outs
        x_ref, g_ref = x_in, g_in
        for parts, chains, whole_ref in ((r_parts, REDUCE_CHAINS, r_ref), (e_parts, EXPAND_CHAINS, e_ref)):
            for part, rows in placed(parts, chains, role):
                whole_ref[rows, :] = part[...]
    else:
        r_in, e_in, keep_ref, send_ref, zh_ref, zl_ref, slope_ref, r_ref, e_ref, x_ref, *later, g_ref, sems = refs
        moves = []
        for columns in in_columns(x_ref.shape[1]):
            moves += [(r_in.at[:, columns], r_ref.at[:, columns]), (x_in.at[0, :, columns], x_ref.at[:, columns])]
        early = len(moves)
        moves += [(e_in, e_ref), (g_in.at[0], g_ref)]
        moves += [(source.at[1 + i // 2], ref) for i, (source, ref) in enumerate(zip((x_in, g_in) * len(later), later))]
        copies = [pltpu.make_async_copy(source, target, sems.at[i]) for i, (source, target) in enumerate(moves)]
        for copy in copies:
            copy.start()
    width = r_ref.shape[0]
    blocks = in_columns(r_ref.shape[1])
    reduce_scale = 1.0 / math.sqrt(r_ref.shape[1])
    expand_scale = 1.0 / math.sqrt(width)
    pre = None
    for i, columns in enumerate(blocks):
        if not joined:
            copies[2 * i].wait()
            copies[2 * i + 1].wait()
        term = product(parts_of(r_ref[:, columns]), (x_ref[:, columns],), NT)
        pre = term if pre is None else pre + term
    pre = pre * reduce_scale
    sig = jax.nn.sigmoid(pre)
    hidden = pre * sig
    slope_ref[...] = sig * (1.0 + pre * (1.0 - sig))
    hidden_t = halves(hidden)
    store_by_role(role, hidden_t, hidden_high_ref, hidden_low_ref)
    hidden_n = tuple(part.T for part in hidden_t)
    if not joined:
        copies[early].wait()
        copies[early + 1].wait()

    def grads_of(columns):
        summed = x_ref[:, columns].astype(f32) + product(hidden_n, parts_of(e_ref[:, columns]), NN) * expand_scale
        sig = jax.nn.sigmoid(summed)
        grads = halves(g_ref[:, columns].astype(f32) * (sig * (1.0 + summed * (1.0 - sig))))
        zh_ref[:, columns], zl_ref[:, columns] = grads
        return grads

    grads = grads_of(blocks[0])
    for i, columns in enumerate(blocks):
        ahead = grads_of(blocks[i + 1]) if i + 1 < len(blocks) else None
        step = product((hidden_high_ref[...], hidden_low_ref[...]), grads, NN) * (learn_rate * expand_scale)
        step_columns(role, columns, e_ref, step, keep_ref, send_ref)
        grads = ahead
    if not joined:
        for copy in copies[early + 2 :]:
            copy.wait()


def reduce_kernel(x_ref, r_ref, e_ref, zh_ref, zl_ref, slope_ref, keep_ref, send_ref, high_ref, low_ref):
    role = places()[0]
    blocks = in_columns(r_ref.shape[1])
    reduce_scale = 1.0 / math.sqrt(r_ref.shape[1])
    expand_scale = 1.0 / math.sqrt(r_ref.shape[0])
    grad_hidden = None
    for columns in blocks:
        term = product(parts_of(e_ref[:, columns]), (zh_ref[:, columns], zl_ref[:, columns]), NT)
        grad_hidden = term if grad_hidden is None else grad_hidden + term
    store_by_role(role, halves(grad_hidden * expand_scale * slope_ref[...]), high_ref, low_ref)
    for columns in blocks:
        step = product((high_ref[...], low_ref[...]), (x_ref[:, columns],), NN) * (learn_rate * reduce_scale)
        step_columns(role, columns, r_ref, step, keep_ref, send_ref)


def shards(w_reduce, w_expand, inputs, out_grads):
    held = [pltpu.with_memory_space_constraint(array[0, 0], pltpu.HBM) for array in (w_reduce, w_expand, inputs, out_grads)]
    reducing, expanding, inputs, out_grads = held
    iterations, rows, columns = inputs.shape
    width = reducing.shape[0]
    half = jax.ShapeDtypeStruct((width // 2, columns), f32)
    acts = jax.ShapeDtypeStruct((rows, columns), bf16)
    slopes = jax.ShapeDtypeStruct((width, rows), f32)
    hidden_parts = [pltpu.VMEM((width, rows), bf16)] * 2
    for iteration in range(iterations):
        first = iteration == 0
        weights = jax.ShapeDtypeStruct((width, columns), bf16 if first else f32)
        results = pl.pallas_call(
            functools.partial(expand_kernel, not first),
            out_shape=(half, half, acts, acts, slopes, weights, weights) + ((acts,) * (2 * iterations - 1) if first else ()),
            in_specs=[HBM] * 4 if first else [VMEM] * (2 + len(sums_r) + len(sums_e)),
            out_specs=(VMEM,) * (7 + (2 * iterations - 1 if first else 0)),
            scratch_shapes=(
                [pltpu.VMEM((rows, columns), bf16), pltpu.SemaphoreType.DMA((2 * columns // BLOCK + 2 * iterations,))] if first else []
            )
            + hidden_parts,
            compiler_params=LARGE,
        )(*((inputs, out_grads, reducing, expanding) if first else (feats[iteration], grads[iteration], *sums_r, *sums_e)))
        keep_e, send_e, zh, zl, slope, reducing, expanding = results[:7]
        if first:
            feats, grads = (results[7], *results[8::2]), (None, *results[9::2])
        keep_r, send_r = pl.pallas_call(
            reduce_kernel,
            out_shape=(half, half),
            in_specs=[VMEM] * 6,
            out_specs=(VMEM,) * 2,
            scratch_shapes=hidden_parts,
            compiler_params=LARGE,
        )(feats[iteration], reducing, expanding, zh, zl, slope)
        sums_e = sum_over_cube(keep_e, send_e, EXPAND_CHAINS)
        sums_r = sum_over_cube(keep_r, send_r, REDUCE_CHAINS)
    reducing, expanding = store(sums_r, sums_e)
    return reducing[None, None], expanding[None, None]


def solution(mesh):
    in_specs = (
        P("near", "far", None, None),
        P("near", "far", None, None),
        P("near", "far", None, None, None),
        P("near", "far", None, None, None),
    )
    out_specs = (P("near", "far", None, None), P("near", "far", None, None))
    return jax.shard_map(shards, mesh=mesh, in_specs=in_specs, out_specs=out_specs, check_vma=False)
```

```python
import functools
import math

import jax
import jax.numpy as jnp
from jax import lax
from jax.experimental import pallas as pl
from jax.experimental.pallas import tpu as pltpu
from jax.sharding import PartitionSpec as P


learn_rate = 1.0

ORDERS = (
    ((1, 3, 2), (3, 2, 1)),
    ((3, 2, 1), (2, 1, 3)),
    ((1, 3, 2), (2, 1, 3)),
    ((1, 3, 2), (3, 2, 1)),
)
REDUCE_CHAINS = ((1, 4), (2, 4))
EXPAND_CHAINS = ((3, 4), (4, 4))
BITS = 4
BLOCK = 256
VMEM = pl.BlockSpec(memory_space=pltpu.VMEM)
HBM = pl.BlockSpec(memory_space=pltpu.HBM)
SMALL = pltpu.CompilerParams(vmem_limit_bytes=2**20)
LARGE = pltpu.CompilerParams(vmem_limit_bytes=12 * 2**20)
f32, bf16 = jnp.float32, jnp.bfloat16


def bits_of(near, far):
    chip = ((near >> 1) & 1, far & 1, (far >> 1) & 1)
    return ((near & 1) ^ chip[0] ^ chip[1] ^ chip[2],) + chip


def places():
    bits = bits_of(lax.axis_index("near"), lax.axis_index("far"))
    return [bits[0]] + [jnp.where(bits[0] == 0, bits[even[0]], bits[odd[0]]) for even, odd in ORDERS]


def from_partner(values, *bit_of_role):
    nears, fars = lax.axis_size("near"), lax.axis_size("far")
    pairs = []
    for near in range(nears):
        for far in range(fars):
            bit = bit_of_role[bits_of(near, far)[0]]
            to_near = near ^ 1 ^ (2 if bit == 1 else 0)
            to_far = far ^ (1 << (bit - 2)) if bit >= 2 else far
            pairs.append((near * fars + far, to_near * fars + to_far))
    return lax.ppermute(values, ("near", "far"), pairs)


def join_kernel(index, own_ref, rest_ref, out_ref):
    rows = own_ref.shape[0]
    place = places()[index]
    out_ref[pl.ds(pl.multiple_of(place * rows, rows), rows), :] = own_ref[...]
    out_ref[pl.ds(pl.multiple_of((1 - place) * rows, rows), rows), :] = rest_ref[...]


def chain(keep, send, index):
    even, odd = ORDERS[index - 1]

    def exchanged(values, step):
        return from_partner(values, even[step % 3], odd[step % 3])

    own = keep + exchanged(send, 0)
    own = own + exchanged(own, 1)
    own = own + exchanged(own, 2)
    rest = exchanged(own, 3)
    rows, columns = own.shape
    joined = pl.pallas_call(
        functools.partial(join_kernel, index),
        out_shape=jax.ShapeDtypeStruct((2 * rows, columns), f32),
        in_specs=[VMEM, VMEM],
        out_specs=VMEM,
        compiler_params=SMALL,
    )(own, rest)
    return joined, from_partner(joined, 0, 0)


def spans(chains, rows):
    first = 0
    for index, eighths in chains:
        yield index, first, rows * eighths // 8
        first += rows * eighths // 8


def meet_kernel(chains, keep_ref, got_ref, *outs):
    place = places()
    for k, (index, first, rows) in enumerate(spans(chains, keep_ref.shape[0])):
        low, high = pl.ds(first, rows // 2), pl.ds(first + rows // 2, rows // 2)
        stays_low = place[index] == 0
        low, high = keep_ref[low, :] + got_ref[low, :], keep_ref[high, :] + got_ref[high, :]
        outs[2 * k][...] = jnp.where(stays_low, low, high)
        outs[2 * k + 1][...] = jnp.where(stays_low, high, low)


def sum_over_cube(keep, send, chains):
    rows, columns = keep.shape
    counts = [count // 2 for _, _, count in spans(chains, rows) for _ in range(2)]
    got = pltpu.with_memory_space_constraint(from_partner(send, 0, 0), pltpu.VMEM)
    pieces = pl.pallas_call(
        functools.partial(meet_kernel, chains),
        out_shape=[jax.ShapeDtypeStruct((count, columns), f32) for count in counts],
        in_specs=[VMEM, VMEM],
        out_specs=[VMEM] * len(counts),
        compiler_params=SMALL,
    )(keep, got)
    parts = [chain(pieces[2 * k], pieces[2 * k + 1], index) for k, (index, _) in enumerate(chains)]
    return [own for own, over in parts] + [over for own, over in parts]


def placed(parts, chains, role):
    rows = sum(part.shape[0] for part in parts) // 2
    firsts = [first for _, first, _ in spans(chains, rows)]
    for i, part in enumerate(parts):
        place = role if i < len(chains) else 1 - role
        yield part, pl.ds(pl.multiple_of(place * rows + firsts[i % len(chains)], 16), part.shape[0])


def store_kernel(chains, *refs):
    *parts, out_ref, sems = refs
    moves = [(part, out_ref.at[rows, :]) for part, rows in placed(parts, chains, places()[0])]
    copies = [pltpu.make_async_copy(source, target, sems.at[i]) for i, (source, target) in enumerate(moves)]
    for copy in copies:
        copy.start()
    for copy in copies:
        copy.wait()


def store(parts, chains):
    return pl.pallas_call(
        functools.partial(store_kernel, chains),
        out_shape=jax.ShapeDtypeStruct((sum(part.shape[0] for part in parts), parts[0].shape[1]), f32),
        in_specs=[VMEM] * len(parts),
        out_specs=HBM,
        scratch_shapes=[pltpu.SemaphoreType.DMA((len(parts),))],
        compiler_params=SMALL,
    )(*parts)


def halves(values):
    high = values.astype(bf16)
    return high, (values - high.astype(f32)).astype(bf16)


def product(left, right, contract):
    total = None
    for i, a in enumerate(left):
        for j, b in enumerate(right):
            if i + j < 2:
                term = lax.dot_general(a, b, (contract, ((), ())), preferred_element_type=f32)
                total = term if total is None else total + term
    return total


def parts_of(values):
    return (values,) if values.dtype == bf16 else halves(values)


NN = ((1,), (0,))
NT = ((1,), (1,))


def in_columns(columns):
    return [pl.ds(start, BLOCK) for start in range(0, columns, BLOCK)]


def store_by_role(role, values, *refs):
    rows = values[0].shape[0] // 2
    for part, ref in zip(values, refs):
        ref[pl.ds(pl.multiple_of(role * rows, rows), rows), :] = part[:rows]
        ref[pl.ds(pl.multiple_of((1 - role) * rows, rows), rows), :] = part[rows:]


def step_columns(role, columns, weights_ref, step, keep_ref, send_ref):
    rows = keep_ref.shape[0]
    for i, (place, ref) in enumerate(((role, keep_ref), (1 - role, send_ref))):
        old = weights_ref[pl.ds(pl.multiple_of(place * rows, rows), rows), columns].astype(f32)
        ref[:, columns] = (old - step[i * rows : (i + 1) * rows]) * (0.5**BITS)


def put_together(parts, chains, whole_ref):
    for part, rows in placed(parts, chains, places()[0]):
        whole_ref[rows, :] = part[...]


def start_copies(moves, sems):
    copies = [pltpu.make_async_copy(source, target, sems.at[i]) for i, (source, target) in enumerate(moves)]
    for copy in copies:
        copy.start()
    return copies


def hidden_of(r_ref, x_ref, outs, arrived):
    slope_ref, high_t_ref, low_t_ref, high_ref, low_ref = outs
    pre = None
    for i, columns in enumerate(in_columns(r_ref.shape[1])):
        arrived(i)
        term = product(parts_of(r_ref[:, columns]), (x_ref[:, columns],), NT)
        pre = term if pre is None else pre + term
    pre = pre * (1.0 / math.sqrt(r_ref.shape[1]))
    sig = jax.nn.sigmoid(pre)
    slope_ref[...] = sig * (1.0 + pre * (1.0 - sig))
    hidden = halves(pre * sig)
    store_by_role(places()[0], hidden, high_t_ref, low_t_ref)
    high_ref[...], low_ref[...] = (part.T for part in hidden)


def first_hidden_kernel(x_in, g_in, r_in, e_in, *refs):
    outs, (r_ref, e_ref), acts_refs, sems = refs[:5], refs[5:7], refs[7:-1], refs[-1]
    moves = []
    for columns in in_columns(r_ref.shape[1]):
        moves += [(r_in.at[:, columns], r_ref.at[:, columns]), (x_in.at[0, :, columns], acts_refs[0].at[:, columns])]
    early = len(moves)
    later = [(source.at[i // 2], ref) for i, (source, ref) in enumerate(zip((x_in, g_in) * len(acts_refs), acts_refs))]
    copies = start_copies(moves + [(e_in, e_ref)] + later[1:], sems)

    def arrived(i):
        copies[2 * i].wait()
        copies[2 * i + 1].wait()

    hidden_of(r_ref, acts_refs[0], outs, arrived)
    for copy in copies[early:]:
        copy.wait()


def hidden_kernel(x_ref, *refs):
    count = 2 * len(REDUCE_CHAINS)
    parts, outs, r_ref = refs[:count], refs[count:-1], refs[-1]
    put_together(parts, REDUCE_CHAINS, r_ref)
    hidden_of(r_ref, x_ref, outs, lambda i: None)


def reduce_kernel(joined, x_ref, g_ref, r_ref, slope_ref, hidden_high_ref, hidden_low_ref, *refs):
    if joined:
        *parts, keep_ref, send_ref, zh_ref, zl_ref, e_ref, high_ref, low_ref = refs
        put_together(parts, EXPAND_CHAINS, e_ref)
    else:
        e_ref, keep_ref, send_ref, zh_ref, zl_ref, high_ref, low_ref = refs
    role = places()[0]
    blocks = in_columns(r_ref.shape[1])
    reduce_scale = 1.0 / math.sqrt(r_ref.shape[1])
    expand_scale = 1.0 / math.sqrt(r_ref.shape[0])
    hidden = hidden_high_ref[...], hidden_low_ref[...]

    def grads_of(columns):
        weights = parts_of(e_ref[:, columns])
        summed = x_ref[:, columns].astype(f32) + product(hidden, weights, NN) * expand_scale
        sig = jax.nn.sigmoid(summed)
        grads = halves(g_ref[:, columns].astype(f32) * (sig * (1.0 + summed * (1.0 - sig))))
        zh_ref[:, columns], zl_ref[:, columns] = grads
        return weights, grads

    grad_hidden = None
    upcoming = grads_of(blocks[0])
    for i in range(len(blocks)):
        weights, grads = upcoming
        upcoming = grads_of(blocks[i + 1]) if i + 1 < len(blocks) else None
        term = product(weights, grads, NT)
        grad_hidden = term if grad_hidden is None else grad_hidden + term
    store_by_role(role, halves(grad_hidden * expand_scale * slope_ref[...]), high_ref, low_ref)
    for columns in blocks:
        step = product((high_ref[...], low_ref[...]), (x_ref[:, columns],), NN) * (learn_rate * reduce_scale)
        step_columns(role, columns, r_ref, step, keep_ref, send_ref)


def expand_kernel(e_ref, zh_ref, zl_ref, hidden_high_ref, hidden_low_ref, keep_ref, send_ref):
    role = places()[0]
    expand_scale = 1.0 / math.sqrt(e_ref.shape[0])
    for columns in in_columns(e_ref.shape[1]):
        grads = zh_ref[:, columns], zl_ref[:, columns]
        step = product((hidden_high_ref[...], hidden_low_ref[...]), grads, NN) * (learn_rate * expand_scale)
        step_columns(role, columns, e_ref, step, keep_ref, send_ref)


def shards(w_reduce, w_expand, inputs, out_grads):
    held = [pltpu.with_memory_space_constraint(array[0, 0], pltpu.HBM) for array in (inputs, out_grads, w_reduce, w_expand)]
    iterations, rows, columns = inputs.shape[2:]
    width = w_reduce.shape[2]
    half = jax.ShapeDtypeStruct((width // 2, columns), f32)
    acts = jax.ShapeDtypeStruct((rows, columns), bf16)
    hidden_shapes = (
        [jax.ShapeDtypeStruct((width, rows), f32)]
        + [jax.ShapeDtypeStruct((width, rows), bf16)] * 2
        + [jax.ShapeDtypeStruct((rows, width), bf16)] * 2
    )
    weights = jax.ShapeDtypeStruct((width, columns), f32)
    narrow = jax.ShapeDtypeStruct((width, columns), bf16)
    results = pl.pallas_call(
        first_hidden_kernel,
        out_shape=hidden_shapes + [narrow] * 2 + [acts] * (2 * iterations),
        in_specs=[HBM] * 4,
        out_specs=[VMEM] * (7 + 2 * iterations),
        scratch_shapes=[pltpu.SemaphoreType.DMA((2 * columns // BLOCK + 2 * iterations,))],
        compiler_params=LARGE,
        name="hidden_0",
    )(*held)
    hidden, (reducing, expanding), acts_of = results[:5], results[5:7], results[7:]
    for iteration in range(iterations):
        first, last = iteration == 0, iteration == iterations - 1
        feats, grads = acts_of[2 * iteration : 2 * iteration + 2]
        slope, high_t, low_t, high, low = hidden
        keep_r, send_r, zh, zl, *joined = pl.pallas_call(
            functools.partial(reduce_kernel, not first),
            out_shape=[half, half, acts, acts] + ([] if first else [weights]),
            in_specs=[VMEM] * (7 if first else 6 + len(expanding)),
            out_specs=[VMEM] * (4 if first else 5),
            scratch_shapes=[pltpu.VMEM((width, rows), bf16)] * 2,
            compiler_params=LARGE,
        )(feats, grads, reducing, slope, high, low, *([expanding] if first else expanding))
        keep_e, send_e = pl.pallas_call(
            expand_kernel, out_shape=[half, half], in_specs=[VMEM] * 5, out_specs=[VMEM] * 2, compiler_params=LARGE
        )(expanding if first else joined[0], zh, zl, high_t, low_t)
        sums_r = sum_over_cube(keep_r, send_r, REDUCE_CHAINS)
        expanding = sum_over_cube(keep_e, send_e, EXPAND_CHAINS)
        if last:
            new_reduce = store(sums_r, REDUCE_CHAINS)
        else:
            *hidden, reducing = pl.pallas_call(
                hidden_kernel,
                out_shape=hidden_shapes + [weights],
                in_specs=[VMEM] * (1 + len(sums_r)),
                out_specs=[VMEM] * 6,
                compiler_params=LARGE,
            )(acts_of[2 * iteration + 2], *sums_r)
    return new_reduce[None, None], store(expanding, EXPAND_CHAINS)[None, None]


def solution(mesh):
    in_specs = (
        P("near", "far", None, None),
        P("near", "far", None, None),
        P("near", "far", None, None, None),
        P("near", "far", None, None, None),
    )
    out_specs = (P("near", "far", None, None), P("near", "far", None, None))
    return jax.shard_map(shards, mesh=mesh, in_specs=in_specs, out_specs=out_specs, check_vma=False)
```

```python
import functools
import math

import jax
import jax.numpy as jnp
from jax import lax
from jax.experimental import pallas as pl
from jax.experimental.pallas import tpu as pltpu
from jax.sharding import PartitionSpec as P


learn_rate = 1.0

ORDERS = (
    ((1, 3, 2), (3, 2, 1)),
    ((2, 3, 1), (2, 1, 3)),
    ((1, 3, 2), (3, 2, 1)),
    ((1, 2, 3), (2, 1, 3)),
)
REDUCE_CHAINS = ((1, 4), (2, 4))
EXPAND_CHAINS = ((3, 4), (4, 4))
BITS = 4
BLOCK = 256
VMEM = pl.BlockSpec(memory_space=pltpu.VMEM)
HBM = pl.BlockSpec(memory_space=pltpu.HBM)
SMALL = pltpu.CompilerParams(vmem_limit_bytes=2**20)
LARGE = pltpu.CompilerParams(vmem_limit_bytes=12 * 2**20)
f32, bf16 = jnp.float32, jnp.bfloat16


def bits_of(near, far):
    chip = ((near >> 1) & 1, far & 1, (far >> 1) & 1)
    return ((near & 1) ^ chip[0] ^ chip[1] ^ chip[2],) + chip


def places():
    bits = bits_of(lax.axis_index("near"), lax.axis_index("far"))
    return [bits[0]] + [jnp.where(bits[0] == 0, bits[even[0]], bits[odd[0]]) for even, odd in ORDERS]


def from_partner(values, *bit_of_role):
    nears, fars = lax.axis_size("near"), lax.axis_size("far")
    pairs = []
    for near in range(nears):
        for far in range(fars):
            bit = bit_of_role[bits_of(near, far)[0]]
            to_near = near ^ 1 ^ (2 if bit == 1 else 0)
            to_far = far ^ (1 << (bit - 2)) if bit >= 2 else far
            pairs.append((near * fars + far, to_near * fars + to_far))
    return lax.ppermute(values, ("near", "far"), pairs)


def join_kernel(index, own_ref, rest_ref, out_ref):
    rows = own_ref.shape[0]
    place = places()[index]
    out_ref[pl.ds(pl.multiple_of(place * rows, rows), rows), :] = own_ref[...]
    out_ref[pl.ds(pl.multiple_of((1 - place) * rows, rows), rows), :] = rest_ref[...]


def chain(keep, send, index):
    even, odd = ORDERS[index - 1]

    def exchanged(values, step):
        return from_partner(values, even[step % 3], odd[step % 3])

    own = keep + exchanged(send, 0)
    own = own + exchanged(own, 1)
    own = own + exchanged(own, 2)
    rest = exchanged(own, 3)
    rows, columns = own.shape
    joined = pl.pallas_call(
        functools.partial(join_kernel, index),
        out_shape=jax.ShapeDtypeStruct((2 * rows, columns), f32),
        in_specs=[VMEM, VMEM],
        out_specs=VMEM,
        compiler_params=SMALL,
    )(own, rest)
    return joined, from_partner(joined, 0, 0)


def spans(chains, rows):
    first = 0
    for index, eighths in chains:
        yield index, first, rows * eighths // 8
        first += rows * eighths // 8


def meet_kernel(chains, keep_ref, got_ref, *outs):
    place = places()
    for k, (index, first, rows) in enumerate(spans(chains, keep_ref.shape[0])):
        low, high = pl.ds(first, rows // 2), pl.ds(first + rows // 2, rows // 2)
        stays_low = place[index] == 0
        low, high = keep_ref[low, :] + got_ref[low, :], keep_ref[high, :] + got_ref[high, :]
        outs[2 * k][...] = jnp.where(stays_low, low, high)
        outs[2 * k + 1][...] = jnp.where(stays_low, high, low)


def sum_over_cube(keep, send, chains):
    rows, columns = keep.shape
    counts = [count // 2 for _, _, count in spans(chains, rows) for _ in range(2)]
    got = pltpu.with_memory_space_constraint(from_partner(send, 0, 0), pltpu.VMEM)
    pieces = pl.pallas_call(
        functools.partial(meet_kernel, chains),
        out_shape=[jax.ShapeDtypeStruct((count, columns), f32) for count in counts],
        in_specs=[VMEM, VMEM],
        out_specs=[VMEM] * len(counts),
        compiler_params=SMALL,
    )(keep, got)
    parts = [chain(pieces[2 * k], pieces[2 * k + 1], index) for k, (index, _) in enumerate(chains)]
    return [own for own, over in parts] + [over for own, over in parts]


def row_span(chains, rows, i, role):
    _, first, count = list(spans(chains, rows))[i % len(chains)]
    place = role if i < len(chains) else 1 - role
    return pl.ds(pl.multiple_of(place * rows + first, 16), count)


def start_copies(moves, sems):
    copies = [pltpu.make_async_copy(source, target, sems.at[i]) for i, (source, target) in enumerate(moves)]
    for copy in copies:
        copy.start()
    return copies


def store_kernel(groups, *refs):
    *refs, sems = refs
    outs = refs[-len(groups) :]
    moves = []
    for (chains, rows, which), out_ref in zip(groups, outs):
        parts, refs = refs[: len(which)], refs[len(which) :]
        for i, part in zip(which, parts):
            moves.append((part, out_ref.at[row_span(chains, rows, i, places()[0]), :]))
    for copy in start_copies(moves, sems):
        copy.wait()


def store(groups, onto=()):
    parts = [part for group in groups for part in group[0]]
    columns = parts[0].shape[1]
    counted = [(chains, rows, which) for _, chains, which, rows in groups]
    return pl.pallas_call(
        functools.partial(store_kernel, counted),
        out_shape=[jax.ShapeDtypeStruct((2 * rows, columns), f32) for _, _, _, rows in groups],
        in_specs=[VMEM] * len(parts) + [HBM] * len(onto),
        out_specs=[HBM] * len(groups),
        scratch_shapes=[pltpu.SemaphoreType.DMA((len(parts),))],
        input_output_aliases={len(parts) + i: i for i in range(len(onto))},
        compiler_params=SMALL,
    )(*parts, *onto)


def halves(values):
    high = values.astype(bf16)
    return high, (values - high.astype(f32)).astype(bf16)


def product(left, right, contract):
    total = None
    for i, a in enumerate(left):
        for j, b in enumerate(right):
            if i + j < 2:
                term = lax.dot_general(a, b, (contract, ((), ())), preferred_element_type=f32)
                total = term if total is None else total + term
    return total


def parts_of(values):
    return (values,) if values.dtype == bf16 else halves(values)


NN = ((1,), (0,))
NT = ((1,), (1,))


def in_columns(columns):
    return [pl.ds(start, BLOCK) for start in range(0, columns, BLOCK)]


def store_by_role(role, values, *refs):
    rows = values[0].shape[0] // 2
    for part, ref in zip(values, refs):
        ref[pl.ds(pl.multiple_of(role * rows, rows), rows), :] = part[:rows]
        ref[pl.ds(pl.multiple_of((1 - role) * rows, rows), rows), :] = part[rows:]


def step_columns(role, columns, weights_ref, step, keep_ref, send_ref):
    rows = keep_ref.shape[0]
    for i, (place, ref) in enumerate(((role, keep_ref), (1 - role, send_ref))):
        old = weights_ref[pl.ds(pl.multiple_of(place * rows, rows), rows), columns].astype(f32)
        ref[:, columns] = (old - step[i * rows : (i + 1) * rows]) * (0.5**BITS)


def put_together(parts, chains, whole_ref):
    for i, part in enumerate(parts):
        whole_ref[row_span(chains, whole_ref.shape[0] // 2, i, places()[0]), :] = part[...]


def hidden_of(r_ref, x_ref, outs, arrived):
    slope_ref, high_t_ref, low_t_ref, high_ref, low_ref = outs
    pre = None
    for i, columns in enumerate(in_columns(r_ref.shape[1])):
        arrived(i)
        term = product(parts_of(r_ref[:, columns]), (x_ref[:, columns],), NT)
        pre = term if pre is None else pre + term
    pre = pre * (1.0 / math.sqrt(r_ref.shape[1]))
    sig = jax.nn.sigmoid(pre)
    slope_ref[...] = sig * (1.0 + pre * (1.0 - sig))
    hidden = halves(pre * sig)
    store_by_role(places()[0], hidden, high_t_ref, low_t_ref)
    high_ref[...], low_ref[...] = (part.T for part in hidden)


def first_hidden_kernel(x_in, g_in, r_in, e_in, *refs):
    outs, (r_ref, e_ref, x_ref, g_ref, sems) = refs[:5], refs[5:]
    moves = []
    for columns in in_columns(r_ref.shape[1]):
        moves += [(r_in.at[:, columns], r_ref.at[:, columns]), (x_in.at[0, :, columns], x_ref.at[:, columns])]
    copies = start_copies(moves + [(e_in, e_ref), (g_in.at[0], g_ref)], sems)

    def arrived(i):
        copies[2 * i].wait()
        copies[2 * i + 1].wait()

    hidden_of(r_ref, x_ref, outs, arrived)
    for copy in copies[len(moves) :]:
        copy.wait()


def hidden_kernel(x_ref, *refs):
    count = 2 * len(REDUCE_CHAINS)
    parts, outs, r_ref = refs[:count], refs[count:-1], refs[-1]
    put_together(parts, REDUCE_CHAINS, r_ref)
    hidden_of(r_ref, x_ref, outs, lambda i: None)


def reduce_kernel(joined, upcoming, x_ref, g_ref, r_ref, slope_ref, hidden_high_ref, hidden_low_ref, *refs):
    copies = []
    if upcoming is not None:
        x_in, g_in, *refs, next_x_ref, next_g_ref, high_ref, low_ref, sems = refs
        copies = start_copies([(x_in.at[upcoming], next_x_ref), (g_in.at[upcoming], next_g_ref)], sems)
        refs = [*refs, high_ref, low_ref]
    if joined:
        *parts, keep_ref, send_ref, zh_ref, zl_ref, e_ref, high_ref, low_ref = refs
        put_together(parts, EXPAND_CHAINS, e_ref)
    else:
        e_ref, keep_ref, send_ref, zh_ref, zl_ref, high_ref, low_ref = refs
    role = places()[0]
    blocks = in_columns(r_ref.shape[1])
    reduce_scale = 1.0 / math.sqrt(r_ref.shape[1])
    expand_scale = 1.0 / math.sqrt(r_ref.shape[0])
    hidden = hidden_high_ref[...], hidden_low_ref[...]

    def grads_of(columns):
        weights = parts_of(e_ref[:, columns])
        summed = x_ref[:, columns].astype(f32) + product(hidden, weights, NN) * expand_scale
        sig = jax.nn.sigmoid(summed)
        grads = halves(g_ref[:, columns].astype(f32) * (sig * (1.0 + summed * (1.0 - sig))))
        zh_ref[:, columns], zl_ref[:, columns] = grads
        return weights, grads

    grad_hidden = None
    upcoming = grads_of(blocks[0])
    for i in range(len(blocks)):
        weights, grads = upcoming
        upcoming = grads_of(blocks[i + 1]) if i + 1 < len(blocks) else None
        term = product(weights, grads, NT)
        grad_hidden = term if grad_hidden is None else grad_hidden + term
    store_by_role(role, halves(grad_hidden * expand_scale * slope_ref[...]), high_ref, low_ref)
    for columns in blocks:
        step = product((high_ref[...], low_ref[...]), (x_ref[:, columns],), NN) * (learn_rate * reduce_scale)
        step_columns(role, columns, r_ref, step, keep_ref, send_ref)
    for copy in copies:
        copy.wait()


def expand_kernel(e_ref, zh_ref, zl_ref, hidden_high_ref, hidden_low_ref, keep_ref, send_ref):
    role = places()[0]
    expand_scale = 1.0 / math.sqrt(e_ref.shape[0])
    for columns in in_columns(e_ref.shape[1]):
        grads = zh_ref[:, columns], zl_ref[:, columns]
        step = product((hidden_high_ref[...], hidden_low_ref[...]), grads, NN) * (learn_rate * expand_scale)
        step_columns(role, columns, e_ref, step, keep_ref, send_ref)


def shards(w_reduce, w_expand, inputs, out_grads):
    held = [pltpu.with_memory_space_constraint(array[0, 0], pltpu.HBM) for array in (inputs, out_grads, w_reduce, w_expand)]
    iterations, rows, columns = inputs.shape[2:]
    width = w_reduce.shape[2]
    half = jax.ShapeDtypeStruct((width // 2, columns), f32)
    acts = jax.ShapeDtypeStruct((rows, columns), bf16)
    hidden_shapes = (
        [jax.ShapeDtypeStruct((width, rows), f32)]
        + [jax.ShapeDtypeStruct((width, rows), bf16)] * 2
        + [jax.ShapeDtypeStruct((rows, width), bf16)] * 2
    )
    weights = jax.ShapeDtypeStruct((width, columns), f32)
    narrow = jax.ShapeDtypeStruct((width, columns), bf16)
    *hidden, reducing, expanding, feats, grads = pl.pallas_call(
        first_hidden_kernel,
        out_shape=hidden_shapes + [narrow] * 2 + [acts] * 2,
        in_specs=[HBM] * 4,
        out_specs=[VMEM] * 9,
        scratch_shapes=[pltpu.SemaphoreType.DMA((2 * columns // BLOCK + 2,))],
        compiler_params=LARGE,
        name="hidden_0",
    )(*held)
    for iteration in range(iterations):
        first, last = iteration == 0, iteration == iterations - 1
        slope, high_t, low_t, high, low = hidden
        weights_in = [expanding] if first else expanding
        keep_r, send_r, zh, zl, *more = pl.pallas_call(
            functools.partial(reduce_kernel, not first, None if last else iteration + 1),
            out_shape=[half, half, acts, acts] + ([] if first else [weights]) + ([] if last else [acts] * 2),
            in_specs=[VMEM] * 6 + ([] if last else [HBM] * 2) + [VMEM] * len(weights_in),
            out_specs=[VMEM] * (4 + (not first) + 2 * (not last)),
            scratch_shapes=[pltpu.VMEM((width, rows), bf16)] * 2 + ([] if last else [pltpu.SemaphoreType.DMA((2,))]),
            compiler_params=LARGE,
        )(feats, grads, reducing, slope, high, low, *([] if last else held[:2]), *weights_in)
        if not first:
            expanding = more.pop(0)
        if not last:
            feats, grads = more
        keep_e, send_e = pl.pallas_call(
            expand_kernel, out_shape=[half, half], in_specs=[VMEM] * 5, out_specs=[VMEM] * 2, compiler_params=LARGE
        )(expanding, zh, zl, high_t, low_t)
        sums_r = sum_over_cube(keep_r, send_r, REDUCE_CHAINS)
        expanding = sum_over_cube(keep_e, send_e, EXPAND_CHAINS)
        if last:
            own = tuple(range(len(EXPAND_CHAINS)))
            groups = [
                (sums_r, REDUCE_CHAINS, tuple(range(len(sums_r))), width // 2),
                ([expanding[i] for i in own], EXPAND_CHAINS, own, width // 2),
            ]
            new_reduce, new_expand = store(groups)
        else:
            *hidden, reducing = pl.pallas_call(
                hidden_kernel,
                out_shape=hidden_shapes + [weights],
                in_specs=[VMEM] * (1 + len(sums_r)),
                out_specs=[VMEM] * 6,
                compiler_params=LARGE,
            )(feats, *sums_r)
    over = tuple(range(len(EXPAND_CHAINS), len(expanding)))
    (new_expand,) = store([([expanding[i] for i in over], EXPAND_CHAINS, over, width // 2)], [new_expand])
    return new_reduce[None, None], new_expand[None, None]


def solution(mesh):
    in_specs = (
        P("near", "far", None, None),
        P("near", "far", None, None),
        P("near", "far", None, None, None),
        P("near", "far", None, None, None),
    )
    out_specs = (P("near", "far", None, None), P("near", "far", None, None))
    return jax.shard_map(shards, mesh=mesh, in_specs=in_specs, out_specs=out_specs, check_vma=False)
```

```python
import functools
import math

import jax
import jax.numpy as jnp
from jax import lax
from jax.experimental import pallas as pl
from jax.experimental.pallas import tpu as pltpu
from jax.sharding import PartitionSpec as P


learn_rate = 1.0

ORDERS = (
    ((1, 3, 2), (3, 2, 1)),
    ((2, 3, 1), (2, 1, 3)),
    ((1, 3, 2), (3, 2, 1)),
    ((1, 2, 3), (2, 1, 3)),
)
REDUCE_CHAINS = ((1, 4), (2, 4))
EXPAND_CHAINS = ((3, 4), (4, 4))
BITS = 4
BLOCK = 256
VMEM = pl.BlockSpec(memory_space=pltpu.VMEM)
HBM = pl.BlockSpec(memory_space=pltpu.HBM)
SMALL = pltpu.CompilerParams(vmem_limit_bytes=2**20)
LARGE = pltpu.CompilerParams(vmem_limit_bytes=12 * 2**20)
f32, bf16 = jnp.float32, jnp.bfloat16


def bits_of(near, far):
    chip = ((near >> 1) & 1, far & 1, (far >> 1) & 1)
    return ((near & 1) ^ chip[0] ^ chip[1] ^ chip[2],) + chip


def places():
    bits = bits_of(lax.axis_index("near"), lax.axis_index("far"))
    return [bits[0]] + [jnp.where(bits[0] == 0, bits[even[0]], bits[odd[0]]) for even, odd in ORDERS]


def from_partner(values, *bit_of_role):
    nears, fars = lax.axis_size("near"), lax.axis_size("far")
    pairs = []
    for near in range(nears):
        for far in range(fars):
            bit = bit_of_role[bits_of(near, far)[0]]
            to_near = near ^ 1 ^ (2 if bit == 1 else 0)
            to_far = far ^ (1 << (bit - 2)) if bit >= 2 else far
            pairs.append((near * fars + far, to_near * fars + to_far))
    return lax.ppermute(values, ("near", "far"), pairs)


def join_kernel(index, own_ref, rest_ref, out_ref):
    rows = own_ref.shape[0]
    place = places()[index]
    out_ref[pl.ds(pl.multiple_of(place * rows, rows), rows), :] = own_ref[...]
    out_ref[pl.ds(pl.multiple_of((1 - place) * rows, rows), rows), :] = rest_ref[...]


def chain(keep, send, index):
    even, odd = ORDERS[index - 1]

    def exchanged(values, step):
        return from_partner(values, even[step % 3], odd[step % 3])

    own = keep + exchanged(send, 0)
    own = own + exchanged(own, 1)
    own = own + exchanged(own, 2)
    rest = exchanged(own, 3)
    rows, columns = own.shape
    joined = pl.pallas_call(
        functools.partial(join_kernel, index),
        out_shape=jax.ShapeDtypeStruct((2 * rows, columns), f32),
        in_specs=[VMEM, VMEM],
        out_specs=VMEM,
        compiler_params=SMALL,
    )(own, rest)
    return joined, from_partner(joined, 0, 0)


def spans(chains, rows):
    first = 0
    for index, eighths in chains:
        yield index, first, rows * eighths // 8
        first += rows * eighths // 8


def meet_kernel(chains, keep_ref, got_ref, *outs):
    place = places()
    for k, (index, first, rows) in enumerate(spans(chains, keep_ref.shape[0])):
        low, high = pl.ds(first, rows // 2), pl.ds(first + rows // 2, rows // 2)
        stays_low = place[index] == 0
        low, high = keep_ref[low, :] + got_ref[low, :], keep_ref[high, :] + got_ref[high, :]
        outs[2 * k][...] = jnp.where(stays_low, low, high)
        outs[2 * k + 1][...] = jnp.where(stays_low, high, low)


def sum_over_cube(keep, send, chains):
    rows, columns = keep.shape
    counts = [count // 2 for _, _, count in spans(chains, rows) for _ in range(2)]
    got = pltpu.with_memory_space_constraint(from_partner(send, 0, 0), pltpu.VMEM)
    pieces = pl.pallas_call(
        functools.partial(meet_kernel, chains),
        out_shape=[jax.ShapeDtypeStruct((count, columns), f32) for count in counts],
        in_specs=[VMEM, VMEM],
        out_specs=[VMEM] * len(counts),
        compiler_params=SMALL,
    )(keep, got)
    parts = [chain(pieces[2 * k], pieces[2 * k + 1], index) for k, (index, _) in enumerate(chains)]
    return [own for own, over in parts] + [over for own, over in parts]


def row_span(chains, rows, i, role):
    _, first, count = list(spans(chains, rows))[i % len(chains)]
    place = role if i < len(chains) else 1 - role
    return pl.ds(pl.multiple_of(place * rows + first, 16), count)


def start_copies(moves, sems):
    copies = [pltpu.make_async_copy(source, target, sems.at[i]) for i, (source, target) in enumerate(moves)]
    for copy in copies:
        copy.start()
    return copies


def store_kernel(groups, *refs):
    *refs, sems = refs
    outs = refs[-len(groups) :]
    moves = []
    for (chains, rows, which), out_ref in zip(groups, outs):
        parts, refs = refs[: len(which)], refs[len(which) :]
        for i, part in zip(which, parts):
            moves.append((part, out_ref.at[row_span(chains, rows, i, places()[0]), :]))
    for copy in start_copies(moves, sems):
        copy.wait()


def store(groups, onto=()):
    parts = [part for group in groups for part in group[0]]
    columns = parts[0].shape[1]
    counted = [(chains, rows, which) for _, chains, which, rows in groups]
    return pl.pallas_call(
        functools.partial(store_kernel, counted),
        out_shape=[jax.ShapeDtypeStruct((2 * rows, columns), f32) for _, _, _, rows in groups],
        in_specs=[VMEM] * len(parts) + [HBM] * len(onto),
        out_specs=[HBM] * len(groups),
        scratch_shapes=[pltpu.SemaphoreType.DMA((len(parts),))],
        input_output_aliases={len(parts) + i: i for i in range(len(onto))},
        compiler_params=SMALL,
    )(*parts, *onto)


def halves(values):
    high = values.astype(bf16)
    return high, (values - high.astype(f32)).astype(bf16)


def product(left, right, contract):
    total = None
    for i, a in enumerate(left):
        for j, b in enumerate(right):
            if i + j < 2:
                term = lax.dot_general(a, b, (contract, ((), ())), preferred_element_type=f32)
                total = term if total is None else total + term
    return total


def parts_of(values):
    return (values,) if values.dtype == bf16 else halves(values)


NN = ((1,), (0,))
NT = ((1,), (1,))


def in_columns(columns):
    return [pl.ds(start, BLOCK) for start in range(0, columns, BLOCK)]


def store_by_role(role, values, *refs):
    rows = values[0].shape[0] // 2
    for part, ref in zip(values, refs):
        ref[pl.ds(pl.multiple_of(role * rows, rows), rows), :] = part[:rows]
        ref[pl.ds(pl.multiple_of((1 - role) * rows, rows), rows), :] = part[rows:]


def step_columns(role, columns, weights_ref, step, keep_ref, send_ref):
    rows = keep_ref.shape[0]
    for i, (place, ref) in enumerate(((role, keep_ref), (1 - role, send_ref))):
        old = weights_ref[pl.ds(pl.multiple_of(place * rows, rows), rows), columns].astype(f32)
        ref[:, columns] = (old - step[i * rows : (i + 1) * rows]) * (0.5**BITS)


def put_together(parts, chains, whole_ref):
    for i, part in enumerate(parts):
        whole_ref[row_span(chains, whole_ref.shape[0] // 2, i, places()[0]), :] = part[...]


def hidden_of(r_ref, x_ref, outs, arrived):
    slope_ref, high_t_ref, low_t_ref, high_ref, low_ref = outs
    pre = None
    for i, columns in enumerate(in_columns(r_ref.shape[1])):
        arrived(i)
        term = product(parts_of(r_ref[:, columns]), (x_ref[:, columns],), NT)
        pre = term if pre is None else pre + term
    pre = pre * (1.0 / math.sqrt(r_ref.shape[1]))
    sig = jax.nn.sigmoid(pre)
    slope_ref[...] = sig * (1.0 + pre * (1.0 - sig))
    hidden = halves(pre * sig)
    store_by_role(places()[0], hidden, high_t_ref, low_t_ref)
    high_ref[...], low_ref[...] = (part.T for part in hidden)


def first_hidden_kernel(x_in, g_in, r_in, e_in, *refs):
    outs, (r_ref, e_ref), acts_refs, sems = refs[:5], refs[5:7], refs[7:-1], refs[-1]
    moves = []
    for columns in in_columns(r_ref.shape[1]):
        moves += [(r_in.at[:, columns], r_ref.at[:, columns]), (x_in.at[0, :, columns], acts_refs[0].at[:, columns])]
    early = len(moves)
    later = [(source.at[i // 2], ref) for i, (source, ref) in enumerate(zip((x_in, g_in) * len(acts_refs), acts_refs))]
    copies = start_copies(moves + [(e_in, e_ref)] + later[1:], sems)

    def arrived(i):
        copies[2 * i].wait()
        copies[2 * i + 1].wait()

    hidden_of(r_ref, acts_refs[0], outs, arrived)
    for copy in copies[early:]:
        copy.wait()


def hidden_kernel(x_ref, *refs):
    count = 2 * len(REDUCE_CHAINS)
    parts, outs, r_ref = refs[:count], refs[count:-1], refs[-1]
    put_together(parts, REDUCE_CHAINS, r_ref)
    hidden_of(r_ref, x_ref, outs, lambda i: None)


def reduce_kernel(joined, x_ref, g_ref, r_ref, slope_ref, hidden_high_ref, hidden_low_ref, *refs):
    if joined:
        *parts, keep_ref, send_ref, zh_ref, zl_ref, e_ref, high_ref, low_ref = refs
        put_together(parts, EXPAND_CHAINS, e_ref)
    else:
        e_ref, keep_ref, send_ref, zh_ref, zl_ref, high_ref, low_ref = refs
    role = places()[0]
    blocks = in_columns(r_ref.shape[1])
    reduce_scale = 1.0 / math.sqrt(r_ref.shape[1])
    expand_scale = 1.0 / math.sqrt(r_ref.shape[0])
    hidden = hidden_high_ref[...], hidden_low_ref[...]

    def grads_of(columns):
        weights = parts_of(e_ref[:, columns])
        summed = x_ref[:, columns].astype(f32) + product(hidden, weights, NN) * expand_scale
        sig = jax.nn.sigmoid(summed)
        grads = halves(g_ref[:, columns].astype(f32) * (sig * (1.0 + summed * (1.0 - sig))))
        zh_ref[:, columns], zl_ref[:, columns] = grads
        return weights, grads

    grad_hidden = None
    upcoming = grads_of(blocks[0])
    for i in range(len(blocks)):
        weights, grads = upcoming
        upcoming = grads_of(blocks[i + 1]) if i + 1 < len(blocks) else None
        term = product(weights, grads, NT)
        grad_hidden = term if grad_hidden is None else grad_hidden + term
    store_by_role(role, halves(grad_hidden * expand_scale * slope_ref[...]), high_ref, low_ref)
    for columns in blocks:
        step = product((high_ref[...], low_ref[...]), (x_ref[:, columns],), NN) * (learn_rate * reduce_scale)
        step_columns(role, columns, r_ref, step, keep_ref, send_ref)


def expand_kernel(e_ref, zh_ref, zl_ref, hidden_high_ref, hidden_low_ref, keep_ref, send_ref):
    role = places()[0]
    expand_scale = 1.0 / math.sqrt(e_ref.shape[0])
    for columns in in_columns(e_ref.shape[1]):
        grads = zh_ref[:, columns], zl_ref[:, columns]
        step = product((hidden_high_ref[...], hidden_low_ref[...]), grads, NN) * (learn_rate * expand_scale)
        step_columns(role, columns, e_ref, step, keep_ref, send_ref)


def shards(w_reduce, w_expand, inputs, out_grads):
    held = [pltpu.with_memory_space_constraint(array[0, 0], pltpu.HBM) for array in (inputs, out_grads, w_reduce, w_expand)]
    iterations, rows, columns = inputs.shape[2:]
    width = w_reduce.shape[2]
    half = jax.ShapeDtypeStruct((width // 2, columns), f32)
    acts = jax.ShapeDtypeStruct((rows, columns), bf16)
    hidden_shapes = (
        [jax.ShapeDtypeStruct((width, rows), f32)]
        + [jax.ShapeDtypeStruct((width, rows), bf16)] * 2
        + [jax.ShapeDtypeStruct((rows, width), bf16)] * 2
    )
    weights = jax.ShapeDtypeStruct((width, columns), f32)
    narrow = jax.ShapeDtypeStruct((width, columns), bf16)
    results = pl.pallas_call(
        first_hidden_kernel,
        out_shape=hidden_shapes + [narrow] * 2 + [acts] * (2 * iterations),
        in_specs=[HBM] * 4,
        out_specs=[VMEM] * (7 + 2 * iterations),
        scratch_shapes=[pltpu.SemaphoreType.DMA((2 * columns // BLOCK + 2 * iterations,))],
        compiler_params=LARGE,
        name="hidden_0",
    )(*held)
    hidden, (reducing, expanding), acts_of = results[:5], results[5:7], results[7:]
    for iteration in range(iterations):
        first, last = iteration == 0, iteration == iterations - 1
        feats, grads = acts_of[2 * iteration : 2 * iteration + 2]
        slope, high_t, low_t, high, low = hidden
        weights_in = [expanding] if first else expanding
        keep_r, send_r, zh, zl, *joined = pl.pallas_call(
            functools.partial(reduce_kernel, not first),
            out_shape=[half, half, acts, acts] + ([] if first else [weights]),
            in_specs=[VMEM] * (6 + len(weights_in)),
            out_specs=[VMEM] * (4 if first else 5),
            scratch_shapes=[pltpu.VMEM((width, rows), bf16)] * 2,
            compiler_params=LARGE,
        )(feats, grads, reducing, slope, high, low, *weights_in)
        if joined:
            (expanding,) = joined
        keep_e, send_e = pl.pallas_call(
            expand_kernel, out_shape=[half, half], in_specs=[VMEM] * 5, out_specs=[VMEM] * 2, compiler_params=LARGE
        )(expanding, zh, zl, high_t, low_t)
        sums_r = sum_over_cube(keep_r, send_r, REDUCE_CHAINS)
        expanding = sum_over_cube(keep_e, send_e, EXPAND_CHAINS)
        if last:
            own = tuple(range(len(EXPAND_CHAINS)))
            groups = [
                (sums_r, REDUCE_CHAINS, tuple(range(len(sums_r))), width // 2),
                ([expanding[i] for i in own], EXPAND_CHAINS, own, width // 2),
            ]
            new_reduce, new_expand = store(groups)
        else:
            *hidden, reducing = pl.pallas_call(
                hidden_kernel,
                out_shape=hidden_shapes + [weights],
                in_specs=[VMEM] * (1 + len(sums_r)),
                out_specs=[VMEM] * 6,
                compiler_params=LARGE,
            )(acts_of[2 * iteration + 2], *sums_r)
    over = tuple(range(len(EXPAND_CHAINS), len(expanding)))
    (new_expand,) = store([([expanding[i] for i in over], EXPAND_CHAINS, over, width // 2)], [new_expand])
    return new_reduce[None, None], new_expand[None, None]


def solution(mesh):
    in_specs = (
        P("near", "far", None, None),
        P("near", "far", None, None),
        P("near", "far", None, None, None),
        P("near", "far", None, None, None),
    )
    out_specs = (P("near", "far", None, None), P("near", "far", None, None))
    return jax.shard_map(shards, mesh=mesh, in_specs=in_specs, out_specs=out_specs, check_vma=False)
```

```python
import functools
import math

import jax
import jax.numpy as jnp
from jax import lax
from jax.experimental import pallas as pl
from jax.experimental.pallas import tpu as pltpu
from jax.sharding import PartitionSpec as P


learn_rate = 1.0

ORDERS = (
    ((2, 3, 1), (3, 1, 2)),
    ((1, 3, 2), (1, 2, 3)),
    ((2, 3, 1), (3, 1, 2)),
    ((2, 1, 3), (1, 2, 3)),
)
REDUCE_CHAINS = ((1, 4), (2, 4))
EXPAND_CHAINS = ((3, 4), (4, 4))
REDUCE_GROUPS = tuple((chain,) for chain in REDUCE_CHAINS)
EXPAND_GROUPS = (EXPAND_CHAINS,)
BITS = 4
BLOCK = 256
VMEM = pl.BlockSpec(memory_space=pltpu.VMEM)
HBM = pl.BlockSpec(memory_space=pltpu.HBM)
SMALL = pltpu.CompilerParams(vmem_limit_bytes=2**20)
LARGE = pltpu.CompilerParams(vmem_limit_bytes=12 * 2**20)
f32, bf16 = jnp.float32, jnp.bfloat16


def bits_of(near, far):
    chip = ((near >> 1) & 1, far & 1, (far >> 1) & 1)
    return ((near & 1) ^ chip[0] ^ chip[1] ^ chip[2],) + chip


def places():
    bits = bits_of(lax.axis_index("near"), lax.axis_index("far"))
    return [bits[0]] + [jnp.where(bits[0] == 0, bits[even[0]], bits[odd[0]]) for even, odd in ORDERS]


def from_partner(values, *bit_of_role):
    nears, fars = lax.axis_size("near"), lax.axis_size("far")
    pairs = []
    for near in range(nears):
        for far in range(fars):
            bit = bit_of_role[bits_of(near, far)[0]]
            to_near = near ^ 1 ^ (2 if bit == 1 else 0)
            to_far = far ^ (1 << (bit - 2)) if bit >= 2 else far
            pairs.append((near * fars + far, to_near * fars + to_far))
    return lax.ppermute(values, ("near", "far"), pairs)


def join_kernel(index, own_ref, rest_ref, out_ref):
    rows = own_ref.shape[0]
    place = places()[index]
    out_ref[pl.ds(pl.multiple_of(place * rows, rows), rows), :] = own_ref[...]
    out_ref[pl.ds(pl.multiple_of((1 - place) * rows, rows), rows), :] = rest_ref[...]


def add_kernel(left_ref, right_ref, out_ref):
    out_ref[...] = left_ref[...] + right_ref[...]


def chain(keep, send, index):
    even, odd = ORDERS[index - 1]

    def exchanged(values, step):
        return from_partner(values, even[step % 3], odd[step % 3])

    got = exchanged(send, 0)
    own = pl.pallas_call(
        add_kernel,
        out_shape=jax.ShapeDtypeStruct(keep.shape, f32),
        in_specs=[VMEM, VMEM],
        out_specs=VMEM,
        compiler_params=SMALL,
    )(keep, got)
    own = own + exchanged(own, 1)
    own = own + exchanged(own, 2)
    rest = exchanged(own, 3)
    rows, columns = own.shape
    joined = pl.pallas_call(
        functools.partial(join_kernel, index),
        out_shape=jax.ShapeDtypeStruct((2 * rows, columns), f32),
        in_specs=[VMEM, VMEM],
        out_specs=VMEM,
        compiler_params=SMALL,
    )(own, rest)
    return joined, from_partner(joined, 0, 0)


def spans(chains, rows):
    first = 0
    for index, eighths in chains:
        yield index, first, rows * eighths // 8
        first += rows * eighths // 8


def meet_kernel(chains, keep_ref, got_ref, *outs):
    place = places()
    first = 0
    for k, (index, _) in enumerate(chains):
        rows = outs[2 * k].shape[0]
        low, high = pl.ds(first, rows), pl.ds(first + rows, rows)
        stays_low = place[index] == 0
        low, high = keep_ref[low, :] + got_ref[low, :], keep_ref[high, :] + got_ref[high, :]
        outs[2 * k][...] = jnp.where(stays_low, low, high)
        outs[2 * k + 1][...] = jnp.where(stays_low, high, low)
        first += 2 * rows


def sum_over_cube(keeps, sends, groups, rows):
    columns = keeps[0].shape[1]
    parts = []
    for chains, keep, send in zip(groups, keeps, sends):
        counts = [rows * eighths // 16 for _, eighths in chains for _ in range(2)]
        got = pltpu.with_memory_space_constraint(from_partner(send, 0, 0), pltpu.VMEM)
        pieces = pl.pallas_call(
            functools.partial(meet_kernel, chains),
            out_shape=[jax.ShapeDtypeStruct((count, columns), f32) for count in counts],
            in_specs=[VMEM, VMEM],
            out_specs=[VMEM] * len(counts),
            compiler_params=SMALL,
        )(keep, got)
        parts += [chain(pieces[2 * k], pieces[2 * k + 1], index) for k, (index, _) in enumerate(chains)]
    return [own for own, over in parts] + [over for own, over in parts]


def row_span(chains, rows, i, role):
    _, first, count = list(spans(chains, rows))[i % len(chains)]
    place = role if i < len(chains) else 1 - role
    return pl.ds(pl.multiple_of(place * rows + first, 16), count)


def start_copies(moves, sems):
    copies = [pltpu.make_async_copy(source, target, sems.at[i]) for i, (source, target) in enumerate(moves)]
    for copy in copies:
        copy.start()
    return copies


def store_kernel(groups, *refs):
    *refs, sems = refs
    outs = refs[-len(groups) :]
    moves = []
    for (chains, rows, which), out_ref in zip(groups, outs):
        parts, refs = refs[: len(which)], refs[len(which) :]
        for i, part in zip(which, parts):
            moves.append((part, out_ref.at[row_span(chains, rows, i, places()[0]), :]))
    for copy in start_copies(moves, sems):
        copy.wait()


def store(groups, onto=()):
    parts = [part for group in groups for part in group[0]]
    columns = parts[0].shape[1]
    counted = [(chains, rows, which) for _, chains, which, rows in groups]
    return pl.pallas_call(
        functools.partial(store_kernel, counted),
        out_shape=[jax.ShapeDtypeStruct((2 * rows, columns), f32) for _, _, _, rows in groups],
        in_specs=[VMEM] * len(parts) + [HBM] * len(onto),
        out_specs=[HBM] * len(groups),
        scratch_shapes=[pltpu.SemaphoreType.DMA((len(parts),))],
        input_output_aliases={len(parts) + i: i for i in range(len(onto))},
        compiler_params=SMALL,
    )(*parts, *onto)


def halves(values):
    high = values.astype(bf16)
    return high, (values - high.astype(f32)).astype(bf16)


def product(left, right, contract):
    total = None
    for i, a in enumerate(left):
        for j, b in enumerate(right):
            if i + j < 2:
                term = lax.dot_general(a, b, (contract, ((), ())), preferred_element_type=f32)
                total = term if total is None else total + term
    return total


def parts_of(values):
    return (values,) if values.dtype == bf16 else halves(values)


NN = ((1,), (0,))
NT = ((1,), (1,))


def in_columns(columns):
    return [pl.ds(start, BLOCK) for start in range(0, columns, BLOCK)]


def store_by_role(role, values, *refs):
    rows = values[0].shape[0] // 2
    for part, ref in zip(values, refs):
        ref[pl.ds(pl.multiple_of(role * rows, rows), rows), :] = part[:rows]
        ref[pl.ds(pl.multiple_of((1 - role) * rows, rows), rows), :] = part[rows:]


def step_columns(role, columns, weights_ref, step, keep_refs, send_refs):
    rows = weights_ref.shape[0] // 2
    for i, (place, refs) in enumerate(((role, keep_refs), (1 - role, send_refs))):
        old = weights_ref[pl.ds(pl.multiple_of(place * rows, rows), rows), columns].astype(f32)
        stepped = (old - step[i * rows : (i + 1) * rows]) * (0.5**BITS)
        first = 0
        for ref in refs:
            ref[:, columns] = stepped[first : first + ref.shape[0]]
            first += ref.shape[0]


def put_together(parts, chains, whole_ref):
    for i, part in enumerate(parts):
        whole_ref[row_span(chains, whole_ref.shape[0] // 2, i, places()[0]), :] = part[...]


def hidden_of(r_ref, x_ref, outs, arrived):
    slope_ref, high_t_ref, low_t_ref, high_ref, low_ref = outs
    pre = None
    for i, columns in enumerate(in_columns(r_ref.shape[1])):
        arrived(i)
        term = product(parts_of(r_ref[:, columns]), (x_ref[:, columns],), NT)
        pre = term if pre is None else pre + term
    pre = pre * (1.0 / math.sqrt(r_ref.shape[1]))
    sig = jax.nn.sigmoid(pre)
    slope_ref[...] = sig * (1.0 + pre * (1.0 - sig))
    hidden = halves(pre * sig)
    store_by_role(places()[0], hidden, high_t_ref, low_t_ref)
    high_ref[...], low_ref[...] = (part.T for part in hidden)


def first_hidden_kernel(x_in, g_in, r_in, e_in, *refs):
    outs, (r_ref, e_ref), acts_refs, sems = refs[:5], refs[5:7], refs[7:-1], refs[-1]
    moves = []
    for columns in in_columns(r_ref.shape[1]):
        moves += [(r_in.at[:, columns], r_ref.at[:, columns]), (x_in.at[0, :, columns], acts_refs[0].at[:, columns])]
    early = len(moves)
    later = [(source.at[i // 2], ref) for i, (source, ref) in enumerate(zip((x_in, g_in) * len(acts_refs), acts_refs))]
    copies = start_copies(moves + [(e_in, e_ref)] + later[1:], sems)

    def arrived(i):
        copies[2 * i].wait()
        copies[2 * i + 1].wait()

    hidden_of(r_ref, acts_refs[0], outs, arrived)
    for copy in copies[early:]:
        copy.wait()


def hidden_kernel(x_ref, *refs):
    count = 2 * len(REDUCE_CHAINS)
    parts, outs, r_ref = refs[:count], refs[count:-1], refs[-1]
    put_together(parts, REDUCE_CHAINS, r_ref)
    hidden_of(r_ref, x_ref, outs, lambda i: None)


def reduce_kernel(joined, x_ref, g_ref, r_ref, slope_ref, hidden_high_ref, hidden_low_ref, *refs):
    if joined:
        *refs, zh_ref, zl_ref, e_ref, high_ref, low_ref = refs
        count = 2 * len(EXPAND_CHAINS)
        put_together(refs[:count], EXPAND_CHAINS, e_ref)
        refs = refs[count:]
    else:
        e_ref, *refs, zh_ref, zl_ref, high_ref, low_ref = refs
    keep_refs, send_refs = refs[: len(REDUCE_GROUPS)], refs[len(REDUCE_GROUPS) :]
    role = places()[0]
    blocks = in_columns(r_ref.shape[1])
    reduce_scale = 1.0 / math.sqrt(r_ref.shape[1])
    expand_scale = 1.0 / math.sqrt(r_ref.shape[0])
    hidden = hidden_high_ref[...], hidden_low_ref[...]

    def grads_of(columns):
        weights = parts_of(e_ref[:, columns])
        summed = x_ref[:, columns].astype(f32) + product(hidden, weights, NN) * expand_scale
        sig = jax.nn.sigmoid(summed)
        grads = halves(g_ref[:, columns].astype(f32) * (sig * (1.0 + summed * (1.0 - sig))))
        zh_ref[:, columns], zl_ref[:, columns] = grads
        return weights, grads

    grad_hidden = None
    upcoming = grads_of(blocks[0])
    for i in range(len(blocks)):
        weights, grads = upcoming
        upcoming = grads_of(blocks[i + 1]) if i + 1 < len(blocks) else None
        term = product(weights, grads, NT)
        grad_hidden = term if grad_hidden is None else grad_hidden + term
    store_by_role(role, halves(grad_hidden * expand_scale * slope_ref[...]), high_ref, low_ref)
    for columns in blocks:
        step = product((high_ref[...], low_ref[...]), (x_ref[:, columns],), NN) * (learn_rate * reduce_scale)
        step_columns(role, columns, r_ref, step, keep_refs, send_refs)


def expand_kernel(e_ref, zh_ref, zl_ref, hidden_high_ref, hidden_low_ref, *refs):
    keep_refs, send_refs = refs[: len(EXPAND_GROUPS)], refs[len(EXPAND_GROUPS) :]
    role = places()[0]
    expand_scale = 1.0 / math.sqrt(e_ref.shape[0])
    for columns in in_columns(e_ref.shape[1]):
        grads = zh_ref[:, columns], zl_ref[:, columns]
        step = product((hidden_high_ref[...], hidden_low_ref[...]), grads, NN) * (learn_rate * expand_scale)
        step_columns(role, columns, e_ref, step, keep_refs, send_refs)


def shards(w_reduce, w_expand, inputs, out_grads):
    held = [pltpu.with_memory_space_constraint(array[0, 0], pltpu.HBM) for array in (inputs, out_grads, w_reduce, w_expand)]
    iterations, rows, columns = inputs.shape[2:]
    width = w_reduce.shape[2]
    halves_r, halves_e = (
        [jax.ShapeDtypeStruct((width // 2 * sum(eighths for _, eighths in chains) // 8, columns), f32) for chains in groups] * 2
        for groups in (REDUCE_GROUPS, EXPAND_GROUPS)
    )
    acts = jax.ShapeDtypeStruct((rows, columns), bf16)
    hidden_shapes = (
        [jax.ShapeDtypeStruct((width, rows), f32)]
        + [jax.ShapeDtypeStruct((width, rows), bf16)] * 2
        + [jax.ShapeDtypeStruct((rows, width), bf16)] * 2
    )
    weights = jax.ShapeDtypeStruct((width, columns), f32)
    narrow = jax.ShapeDtypeStruct((width, columns), bf16)
    results = pl.pallas_call(
        first_hidden_kernel,
        out_shape=hidden_shapes + [narrow] * 2 + [acts] * (2 * iterations),
        in_specs=[HBM] * 4,
        out_specs=[VMEM] * (7 + 2 * iterations),
        scratch_shapes=[pltpu.SemaphoreType.DMA((2 * columns // BLOCK + 2 * iterations,))],
        compiler_params=LARGE,
        name="hidden_0",
    )(*held)
    hidden, (reducing, expanding), acts_of = results[:5], results[5:7], results[7:]
    for iteration in range(iterations):
        first, last = iteration == 0, iteration == iterations - 1
        feats, grads = acts_of[2 * iteration : 2 * iteration + 2]
        slope, high_t, low_t, high, low = hidden
        weights_in = [expanding] if first else expanding
        results = pl.pallas_call(
            functools.partial(reduce_kernel, not first),
            out_shape=halves_r + [acts] * 2 + ([] if first else [weights]),
            in_specs=[VMEM] * (6 + len(weights_in)),
            out_specs=[VMEM] * (len(halves_r) + (2 if first else 3)),
            scratch_shapes=[pltpu.VMEM((width, rows), bf16)] * 2,
            compiler_params=LARGE,
        )(feats, grads, reducing, slope, high, low, *weights_in)
        stepped_r, (zh, zl, *joined) = results[: len(halves_r)], results[len(halves_r) :]
        if joined:
            (expanding,) = joined
        stepped_e = pl.pallas_call(
            expand_kernel,
            out_shape=halves_e,
            in_specs=[VMEM] * 5,
            out_specs=[VMEM] * len(halves_e),
            compiler_params=LARGE,
        )(expanding, zh, zl, high_t, low_t)
        r, e = len(REDUCE_GROUPS), len(EXPAND_GROUPS)
        sums_r = sum_over_cube(stepped_r[:r], stepped_r[r:], REDUCE_GROUPS, width // 2)
        expanding = sum_over_cube(stepped_e[:e], stepped_e[e:], EXPAND_GROUPS, width // 2)
        if last:
            own = tuple(range(len(EXPAND_CHAINS)))
            groups = [
                (sums_r, REDUCE_CHAINS, tuple(range(len(sums_r))), width // 2),
                ([expanding[i] for i in own], EXPAND_CHAINS, own, width // 2),
            ]
            new_reduce, new_expand = store(groups)
        else:
            *hidden, reducing = pl.pallas_call(
                hidden_kernel,
                out_shape=hidden_shapes + [weights],
                in_specs=[VMEM] * (1 + len(sums_r)),
                out_specs=[VMEM] * 6,
                compiler_params=LARGE,
            )(acts_of[2 * iteration + 2], *sums_r)
    over = tuple(range(len(EXPAND_CHAINS), len(expanding)))
    (new_expand,) = store([([expanding[i] for i in over], EXPAND_CHAINS, over, width // 2)], [new_expand])
    return new_reduce[None, None], new_expand[None, None]


def solution(mesh):
    in_specs = (
        P("near", "far", None, None),
        P("near", "far", None, None),
        P("near", "far", None, None, None),
        P("near", "far", None, None, None),
    )
    out_specs = (P("near", "far", None, None), P("near", "far", None, None))
    return jax.shard_map(shards, mesh=mesh, in_specs=in_specs, out_specs=out_specs, check_vma=False)
```

```python
import functools
import math

import jax
import jax.numpy as jnp
from jax import lax
from jax.experimental import pallas as pl
from jax.experimental.pallas import tpu as pltpu
from jax.sharding import PartitionSpec as P


learn_rate = 1.0

ORDERS = (
    ((2, 3, 1), (3, 1, 2)),
    ((1, 3, 2), (1, 2, 3)),
    ((2, 3, 1), (3, 1, 2)),
    ((2, 1, 3), (1, 2, 3)),
)
REDUCE_CHAINS = ((1, 4), (2, 4))
EXPAND_CHAINS = ((3, 4), (4, 4))
REDUCE_GROUPS = tuple((chain,) for chain in REDUCE_CHAINS)
EXPAND_GROUPS = (EXPAND_CHAINS,)
BITS = 4
BLOCK = 256
VMEM = pl.BlockSpec(memory_space=pltpu.VMEM)
HBM = pl.BlockSpec(memory_space=pltpu.HBM)
SMALL = pltpu.CompilerParams(vmem_limit_bytes=2**20)
LARGE = pltpu.CompilerParams(vmem_limit_bytes=12 * 2**20)
f32, bf16 = jnp.float32, jnp.bfloat16


def bits_of(near, far):
    chip = ((near >> 1) & 1, far & 1, (far >> 1) & 1)
    return ((near & 1) ^ chip[0] ^ chip[1] ^ chip[2],) + chip


def places():
    bits = bits_of(lax.axis_index("near"), lax.axis_index("far"))
    return [bits[0]] + [jnp.where(bits[0] == 0, bits[even[0]], bits[odd[0]]) for even, odd in ORDERS]


def from_partner(values, *bit_of_role):
    nears, fars = lax.axis_size("near"), lax.axis_size("far")
    pairs = []
    for near in range(nears):
        for far in range(fars):
            bit = bit_of_role[bits_of(near, far)[0]]
            to_near = near ^ 1 ^ (2 if bit == 1 else 0)
            to_far = far ^ (1 << (bit - 2)) if bit >= 2 else far
            pairs.append((near * fars + far, to_near * fars + to_far))
    return lax.ppermute(values, ("near", "far"), pairs)


def join_kernel(index, own_ref, rest_ref, out_ref):
    rows = own_ref.shape[0]
    place = places()[index]
    out_ref[pl.ds(pl.multiple_of(place * rows, rows), rows), :] = own_ref[...]
    out_ref[pl.ds(pl.multiple_of((1 - place) * rows, rows), rows), :] = rest_ref[...]


def add_kernel(left_ref, right_ref, out_ref):
    out_ref[...] = left_ref[...] + right_ref[...]


def chain(keep, send, index):
    even, odd = ORDERS[index - 1]

    def exchanged(values, step):
        return from_partner(values, even[step % 3], odd[step % 3])

    got = exchanged(send, 0)
    own = pl.pallas_call(
        add_kernel,
        out_shape=jax.ShapeDtypeStruct(keep.shape, f32),
        in_specs=[VMEM, VMEM],
        out_specs=VMEM,
        compiler_params=SMALL,
    )(keep, got)
    own = own + exchanged(own, 1)
    own = own + exchanged(own, 2)
    rest = exchanged(own, 3)
    rows, columns = own.shape
    joined = pl.pallas_call(
        functools.partial(join_kernel, index),
        out_shape=jax.ShapeDtypeStruct((2 * rows, columns), f32),
        in_specs=[VMEM, VMEM],
        out_specs=VMEM,
        compiler_params=SMALL,
    )(own, rest)
    return joined, from_partner(joined, 0, 0)


def spans(chains, rows):
    first = 0
    for index, eighths in chains:
        yield index, first, rows * eighths // 8
        first += rows * eighths // 8


def meet_kernel(chains, keep_ref, got_ref, *outs):
    place = places()
    first = 0
    for k, (index, _) in enumerate(chains):
        rows = outs[2 * k].shape[0]
        low, high = pl.ds(first, rows), pl.ds(first + rows, rows)
        stays_low = place[index] == 0
        low, high = keep_ref[low, :] + got_ref[low, :], keep_ref[high, :] + got_ref[high, :]
        outs[2 * k][...] = jnp.where(stays_low, low, high)
        outs[2 * k + 1][...] = jnp.where(stays_low, high, low)
        first += 2 * rows


def sum_over_cube(keeps, sends, groups, rows):
    columns = keeps[0].shape[1]
    parts = []
    for chains, keep, send in zip(groups, keeps, sends):
        counts = [rows * eighths // 16 for _, eighths in chains for _ in range(2)]
        got = pltpu.with_memory_space_constraint(from_partner(send, 0, 0), pltpu.VMEM)
        pieces = pl.pallas_call(
            functools.partial(meet_kernel, chains),
            out_shape=[jax.ShapeDtypeStruct((count, columns), f32) for count in counts],
            in_specs=[VMEM, VMEM],
            out_specs=[VMEM] * len(counts),
            compiler_params=SMALL,
        )(keep, got)
        parts += [chain(pieces[2 * k], pieces[2 * k + 1], index) for k, (index, _) in enumerate(chains)]
    return [own for own, over in parts] + [over for own, over in parts]


def row_span(chains, rows, i, role):
    _, first, count = list(spans(chains, rows))[i % len(chains)]
    place = role if i < len(chains) else 1 - role
    return pl.ds(pl.multiple_of(place * rows + first, 16), count)


def start_copies(moves, sems):
    copies = [pltpu.make_async_copy(source, target, sems.at[i]) for i, (source, target) in enumerate(moves)]
    for copy in copies:
        copy.start()
    return copies


def store_kernel(groups, *refs):
    *refs, sems = refs
    outs = refs[-len(groups) :]
    moves = []
    for (chains, rows, which), out_ref in zip(groups, outs):
        parts, refs = refs[: len(which)], refs[len(which) :]
        for i, part in zip(which, parts):
            moves.append((part, out_ref.at[row_span(chains, rows, i, places()[0]), :]))
    for copy in start_copies(moves, sems):
        copy.wait()


def store(groups, onto=()):
    parts = [part for group in groups for part in group[0]]
    columns = parts[0].shape[1]
    counted = [(chains, rows, which) for _, chains, which, rows in groups]
    return pl.pallas_call(
        functools.partial(store_kernel, counted),
        out_shape=[jax.ShapeDtypeStruct((2 * rows, columns), f32) for _, _, _, rows in groups],
        in_specs=[VMEM] * len(parts) + [HBM] * len(onto),
        out_specs=[HBM] * len(groups),
        scratch_shapes=[pltpu.SemaphoreType.DMA((len(parts),))],
        input_output_aliases={len(parts) + i: i for i in range(len(onto))},
        compiler_params=SMALL,
    )(*parts, *onto)


def halves(values):
    high = values.astype(bf16)
    return high, (values - high.astype(f32)).astype(bf16)


def product(left, right, contract):
    total = None
    for i, a in enumerate(left):
        for j, b in enumerate(right):
            if i + j < 2:
                term = lax.dot_general(a, b, (contract, ((), ())), preferred_element_type=f32)
                total = term if total is None else total + term
    return total


def parts_of(values):
    return (values,) if values.dtype == bf16 else halves(values)


NN = ((1,), (0,))
NT = ((1,), (1,))


def in_columns(columns):
    return [pl.ds(start, BLOCK) for start in range(0, columns, BLOCK)]


def store_by_role(role, values, *refs):
    rows = values[0].shape[0] // 2
    for part, ref in zip(values, refs):
        ref[pl.ds(pl.multiple_of(role * rows, rows), rows), :] = part[:rows]
        ref[pl.ds(pl.multiple_of((1 - role) * rows, rows), rows), :] = part[rows:]


def step_columns(role, columns, weights_ref, step, keep_refs, send_refs):
    rows = weights_ref.shape[0] // 2
    for i, (place, refs) in enumerate(((role, keep_refs), (1 - role, send_refs))):
        old = weights_ref[pl.ds(pl.multiple_of(place * rows, rows), rows), columns].astype(f32)
        stepped = (old - step[i * rows : (i + 1) * rows]) * (0.5**BITS)
        first = 0
        for ref in refs:
            ref[:, columns] = stepped[first : first + ref.shape[0]]
            first += ref.shape[0]


def put_together(parts, chains, whole_ref):
    for i, part in enumerate(parts):
        whole_ref[row_span(chains, whole_ref.shape[0] // 2, i, places()[0]), :] = part[...]


def hidden_of(r_ref, x_ref, outs, arrived):
    slope_ref, high_t_ref, low_t_ref, high_ref, low_ref = outs
    pre = None
    for i, columns in enumerate(in_columns(r_ref.shape[1])):
        arrived(i)
        term = product(parts_of(r_ref[:, columns]), (x_ref[:, columns],), NT)
        pre = term if pre is None else pre + term
    pre = pre * (1.0 / math.sqrt(r_ref.shape[1]))
    sig = jax.nn.sigmoid(pre)
    slope_ref[...] = sig * (1.0 + pre * (1.0 - sig))
    hidden = halves(pre * sig)
    store_by_role(places()[0], hidden, high_t_ref, low_t_ref)
    high_ref[...], low_ref[...] = (part.T for part in hidden)


def first_hidden_kernel(x_in, g_in, r_in, e_in, *refs):
    outs, (r_ref, e_ref), acts_refs, sems = refs[:5], refs[5:7], refs[7:-1], refs[-1]
    moves = []
    for columns in in_columns(r_ref.shape[1]):
        moves += [(r_in.at[:, columns], r_ref.at[:, columns]), (x_in.at[0, :, columns], acts_refs[0].at[:, columns])]
    early = len(moves)
    later = [(source.at[i // 2], ref) for i, (source, ref) in enumerate(zip((x_in, g_in) * len(acts_refs), acts_refs))]
    copies = start_copies(moves, sems)
    for i, (source, target) in enumerate([(e_in, e_ref)] + later[1:]):
        copies.append(pltpu.make_async_copy(source, target, sems.at[early + i]))

    def arrived(i):
        copies[2 * i].wait()
        copies[2 * i + 1].wait()
        if i == 0:
            for copy in copies[early:]:
                copy.start()

    hidden_of(r_ref, acts_refs[0], outs, arrived)
    for copy in copies[early:]:
        copy.wait()


def hidden_kernel(x_ref, *refs):
    count = 2 * len(REDUCE_CHAINS)
    parts, outs, r_ref = refs[:count], refs[count:-1], refs[-1]
    put_together(parts, REDUCE_CHAINS, r_ref)
    hidden_of(r_ref, x_ref, outs, lambda i: None)


def reduce_kernel(joined, x_ref, g_ref, r_ref, slope_ref, hidden_high_ref, hidden_low_ref, *refs):
    if joined:
        *refs, zh_ref, zl_ref, e_ref, high_ref, low_ref = refs
        count = 2 * len(EXPAND_CHAINS)
        put_together(refs[:count], EXPAND_CHAINS, e_ref)
        refs = refs[count:]
    else:
        e_ref, *refs, zh_ref, zl_ref, high_ref, low_ref = refs
    keep_refs, send_refs = refs[: len(REDUCE_GROUPS)], refs[len(REDUCE_GROUPS) :]
    role = places()[0]
    blocks = in_columns(r_ref.shape[1])
    reduce_scale = 1.0 / math.sqrt(r_ref.shape[1])
    expand_scale = 1.0 / math.sqrt(r_ref.shape[0])
    hidden = hidden_high_ref[...], hidden_low_ref[...]

    def grads_of(columns):
        weights = parts_of(e_ref[:, columns])
        summed = x_ref[:, columns].astype(f32) + product(hidden, weights, NN) * expand_scale
        sig = jax.nn.sigmoid(summed)
        grads = halves(g_ref[:, columns].astype(f32) * (sig * (1.0 + summed * (1.0 - sig))))
        zh_ref[:, columns], zl_ref[:, columns] = grads
        return weights, grads

    grad_hidden = None
    upcoming = grads_of(blocks[0])
    for i in range(len(blocks)):
        weights, grads = upcoming
        upcoming = grads_of(blocks[i + 1]) if i + 1 < len(blocks) else None
        term = product(weights, grads, NT)
        grad_hidden = term if grad_hidden is None else grad_hidden + term
    store_by_role(role, halves(grad_hidden * expand_scale * slope_ref[...]), high_ref, low_ref)
    for columns in blocks:
        step = product((high_ref[...], low_ref[...]), (x_ref[:, columns],), NN) * (learn_rate * reduce_scale)
        step_columns(role, columns, r_ref, step, keep_refs, send_refs)


def expand_kernel(e_ref, zh_ref, zl_ref, hidden_high_ref, hidden_low_ref, *refs):
    keep_refs, send_refs = refs[: len(EXPAND_GROUPS)], refs[len(EXPAND_GROUPS) :]
    role = places()[0]
    expand_scale = 1.0 / math.sqrt(e_ref.shape[0])
    for columns in in_columns(e_ref.shape[1]):
        grads = zh_ref[:, columns], zl_ref[:, columns]
        step = product((hidden_high_ref[...], hidden_low_ref[...]), grads, NN) * (learn_rate * expand_scale)
        step_columns(role, columns, e_ref, step, keep_refs, send_refs)


def shards(w_reduce, w_expand, inputs, out_grads):
    held = [pltpu.with_memory_space_constraint(array[0, 0], pltpu.HBM) for array in (inputs, out_grads, w_reduce, w_expand)]
    iterations, rows, columns = inputs.shape[2:]
    width = w_reduce.shape[2]
    halves_r, halves_e = (
        [jax.ShapeDtypeStruct((width // 2 * sum(eighths for _, eighths in chains) // 8, columns), f32) for chains in groups] * 2
        for groups in (REDUCE_GROUPS, EXPAND_GROUPS)
    )
    acts = jax.ShapeDtypeStruct((rows, columns), bf16)
    hidden_shapes = (
        [jax.ShapeDtypeStruct((width, rows), f32)]
        + [jax.ShapeDtypeStruct((width, rows), bf16)] * 2
        + [jax.ShapeDtypeStruct((rows, width), bf16)] * 2
    )
    weights = jax.ShapeDtypeStruct((width, columns), f32)
    narrow = jax.ShapeDtypeStruct((width, columns), bf16)
    results = pl.pallas_call(
        first_hidden_kernel,
        out_shape=hidden_shapes + [narrow] * 2 + [acts] * (2 * iterations),
        in_specs=[HBM] * 4,
        out_specs=[VMEM] * (7 + 2 * iterations),
        scratch_shapes=[pltpu.SemaphoreType.DMA((2 * columns // BLOCK + 2 * iterations,))],
        compiler_params=LARGE,
        name="hidden_0",
    )(*held)
    hidden, (reducing, expanding), acts_of = results[:5], results[5:7], results[7:]
    for iteration in range(iterations):
        first, last = iteration == 0, iteration == iterations - 1
        feats, grads = acts_of[2 * iteration : 2 * iteration + 2]
        slope, high_t, low_t, high, low = hidden
        weights_in = [expanding] if first else expanding
        results = pl.pallas_call(
            functools.partial(reduce_kernel, not first),
            out_shape=halves_r + [acts] * 2 + ([] if first else [weights]),
            in_specs=[VMEM] * (6 + len(weights_in)),
            out_specs=[VMEM] * (len(halves_r) + (2 if first else 3)),
            scratch_shapes=[pltpu.VMEM((width, rows), bf16)] * 2,
            compiler_params=LARGE,
        )(feats, grads, reducing, slope, high, low, *weights_in)
        stepped_r, (zh, zl, *joined) = results[: len(halves_r)], results[len(halves_r) :]
        if joined:
            (expanding,) = joined
        stepped_e = pl.pallas_call(
            expand_kernel,
            out_shape=halves_e,
            in_specs=[VMEM] * 5,
            out_specs=[VMEM] * len(halves_e),
            compiler_params=LARGE,
        )(expanding, zh, zl, high_t, low_t)
        r, e = len(REDUCE_GROUPS), len(EXPAND_GROUPS)
        sums_r = sum_over_cube(stepped_r[:r], stepped_r[r:], REDUCE_GROUPS, width // 2)
        expanding = sum_over_cube(stepped_e[:e], stepped_e[e:], EXPAND_GROUPS, width // 2)
        if last:
            own = tuple(range(len(EXPAND_CHAINS)))
            groups = [
                (sums_r, REDUCE_CHAINS, tuple(range(len(sums_r))), width // 2),
                ([expanding[i] for i in own], EXPAND_CHAINS, own, width // 2),
            ]
            new_reduce, new_expand = store(groups)
        else:
            *hidden, reducing = pl.pallas_call(
                hidden_kernel,
                out_shape=hidden_shapes + [weights],
                in_specs=[VMEM] * (1 + len(sums_r)),
                out_specs=[VMEM] * 6,
                compiler_params=LARGE,
            )(acts_of[2 * iteration + 2], *sums_r)
    over = tuple(range(len(EXPAND_CHAINS), len(expanding)))
    (new_expand,) = store([([expanding[i] for i in over], EXPAND_CHAINS, over, width // 2)], [new_expand])
    return new_reduce[None, None], new_expand[None, None]


def solution(mesh):
    in_specs = (
        P("near", "far", None, None),
        P("near", "far", None, None),
        P("near", "far", None, None, None),
        P("near", "far", None, None, None),
    )
    out_specs = (P("near", "far", None, None), P("near", "far", None, None))
    return jax.shard_map(shards, mesh=mesh, in_specs=in_specs, out_specs=out_specs, check_vma=False)
```
